512 devices in a mesh: chan: 16 (over y, x), patch: 32 (over z, core).
Axes of the slice: x: 4, y: 4, z: 16, core: 2. Of those that a mesh axis runs over, the one named last changes fastest.
Arguments:
- sky_maps: float32 [64, 393216], P('chan', 'patch')
- mode_vectors: float32 [64, 8], replicated
- pixel_weight: float32 [393216], P('patch'), may hold values from 0.3 to 3
- neighbours: int32 [48, 64, 9], P('chan', 'patch'), may hold values from 0 to 8, as said below
- tile_counts: int32 [48, 64], P('chan', 'patch'), may hold values from 0 to 9, as said below
- pair_bins: int32 [9, 128, 128], replicated, may hold values from 0 to 8, as said below
Outputs:
- correlation: float32 [16, 32, 8, 64, 64], P('chan', 'patch')
- covariance: float32 [64, 64], replicated
The draws below stay inside these ranges and needn't reach their ends.
Inputs may be any that keep to these rules, and one draw needn't show every extreme that they name: `neighbours`: for tile (A, B) the first tile_counts[A, B] entries are distinct offset codes o in ascending order, each naming the tile (A + o // 3 - 1, B + o % 3 - 1), which lies inside the grid and is observed; later entries mean nothing. An observed tile lists code 4 (itself); if a tile lists another, that one lists it back. `tile_counts`: 0 exactly for tiles that are not observed; some tile has 9. `pair_bins`: one table for each offset code, the same for every tile pair with that offset; the value 8 marks a pair beyond the last bin.
All inputs are finite; a program needn't handle non-finite values.
Results may differ from the reference program's by a relative error of at most 0.00075.
Values may be sent and summed in bfloat16 or wider, within the bound.
A program may use at most 64 MiB of HBM per device.

```python
import math
import jax
import jax.numpy as jnp
from jax import lax

NCH = 64
MODES = 8
TILE = 128
NBIN = 8
NBR = 9
TA = 3
TB = 2
NTA = 48
NTB = 64
NPIX = 393216


def mode_table(key):
    return jax.random.normal(jax.random.fold_in(key, 11), (NCH, MODES), jnp.float32)


def draw_mode_vectors(key, part):
    return mode_table(key)


def draw_sky_maps(key, part):
    vectors = mode_table(key)
    key_list = [jax.random.fold_in(key, 20 + number) for number in range(6)]
    amplitude = 5.0 * jax.random.normal(key_list[0], (MODES, NTA * NTB * TILE), jnp.float32)
    foreground = jnp.dot(vectors, amplitude, precision=lax.Precision.HIGHEST, preferred_element_type=jnp.float32)
    gains = jnp.exp(jax.random.uniform(key_list[1], (NCH, 1, 1, 1), jnp.float32, math.log(0.5), math.log(5.0)))
    roughness = jax.random.normal(key_list[2], (NCH, NTA, NTB, TILE), jnp.float32)
    common = jax.random.normal(key_list[3], (1, NTA + 1, NTB + 1), jnp.float32)
    own_part = jax.random.normal(key_list[4], (NCH, NTA + 1, NTB + 1), jnp.float32)
    corner = common + own_part
    level = 0.25 * (corner[:, :-1, :-1] + corner[:, 1:, :-1] + corner[:, :-1, 1:] + corner[:, 1:, 1:])
    row_place = jnp.arange(NTA, dtype=jnp.float32)[:, None] / NTA
    col_place = jnp.arange(NTB, dtype=jnp.float32)[None, :] / NTB
    rising = jnp.exp(math.log(3.0) * (row_place + col_place))
    scatter = jnp.exp(jax.random.uniform(key_list[5], (1, NTA, NTB, TILE), jnp.float32, math.log(0.5), math.log(2.0)))
    signal = gains * rising[None, :, :, None] * (level[:, :, :, None] + 0.6 * roughness * scatter)
    total = foreground.reshape(NCH, NTA, NTB, TILE) + signal
    patch_count = NTB // TB
    total = total.reshape(NCH, NTA, patch_count, TB, TILE).transpose(0, 2, 1, 3, 4)
    return total.reshape(NCH, NTA * NTB * TILE)


def tile_graph(key):
    start_key = jax.random.fold_in(key, 31)
    toss_key = jax.random.fold_in(key, 32)
    drop_key = jax.random.fold_in(key, 33)
    hub_key = jax.random.fold_in(key, 34)
    band_rows = max(NTA // 4, 3)
    band_start = jax.random.randint(start_key, (), 0, NTA - band_rows + 1)
    row_index = jnp.arange(NTA, dtype=jnp.int32)[:, None]
    col_index = jnp.arange(NTB, dtype=jnp.int32)[None, :]
    coin_toss = jax.random.randint(toss_key, (NTA, NTB), 0, 100)
    in_band = (row_index >= band_start) & (row_index < band_start + band_rows)
    observed = (coin_toss < 35) | in_band
    padded = jnp.pad(observed, 1)
    keep_forward = jax.random.randint(drop_key, (NTA, NTB, 4), 0, 100) >= 20
    keep_padded = jnp.pad(keep_forward, ((1, 1), (1, 1), (0, 0)))
    hub_row = band_start + 1
    hub_col = jax.random.randint(hub_key, (), 1, NTB - 1)
    hub_tile = (row_index == hub_row) & (col_index == hub_col)
    hub_padded = jnp.pad(hub_tile, 1)
    live_list = []
    for offset_code in range(9):
        row_shift = offset_code // 3
        col_shift = offset_code % 3
        partner_seen = padded[row_shift:row_shift + NTA, col_shift:col_shift + NTB]
        if offset_code == 4:
            kept = jnp.ones((NTA, NTB), dtype=bool)
        elif offset_code > 4:
            kept = keep_forward[:, :, offset_code - 5]
        else:
            kept = keep_padded[row_shift:row_shift + NTA, col_shift:col_shift + NTB, 3 - offset_code]
        touches = hub_tile | hub_padded[row_shift:row_shift + NTA, col_shift:col_shift + NTB]
        live_list.append(observed & partner_seen & (kept | touches))
    live = jnp.stack(live_list, axis=-1).astype(jnp.int32)
    score = jnp.arange(9, dtype=jnp.int32)[None, None, :] + 9 * (1 - live)
    ordered = jnp.argsort(score, axis=-1, stable=True).astype(jnp.int32)
    counted = jnp.sum(live, axis=-1).astype(jnp.int32)
    return (ordered, counted)


def draw_neighbours(key, part):
    return tile_graph(key)[0]


def draw_tile_counts(key, part):
    return tile_graph(key)[1]


def draw_pair_bins(key, part):
    jitter_key = jax.random.fold_in(key, 41)
    codes = jnp.arange(NBR, dtype=jnp.int32)[:, None, None]
    first = jnp.arange(TILE, dtype=jnp.int32)[None, :, None]
    second = jnp.arange(TILE, dtype=jnp.int32)[None, None, :]
    row_gap = (codes // 3 - 1) * (TILE // 16) + second // 16 - first // 16
    col_gap = (codes % 3 - 1) * 16 + second % 16 - first % 16
    square = row_gap * row_gap + col_gap * col_gap
    geometric = jnp.zeros((NBR, TILE, TILE), jnp.int32)
    for level in range(1, NBIN + 1):
        geometric = geometric + (NBIN * NBIN * square >= 13 * level * (13 * level)).astype(jnp.int32)
    jitter = jax.random.randint(jitter_key, (NBR, TILE, TILE), -1, 2)
    jittered = jnp.clip(geometric + jitter, 0, NBIN - 1)
    return jnp.where(geometric < NBIN, jittered, NBIN).astype(jnp.int32)


def steps_of(key, extent, split, least, largest):
    gain, own = 1.0, jax.random.fold_in(key, 6)
    for dim, shards_of in split:
        steps = jnp.exp(jax.random.uniform(jax.random.fold_in(own, dim), (shards_of,), jnp.float32, least / len(split), largest / len(split)))
        gain = gain * jnp.repeat(steps, extent[dim] // shards_of).reshape([-1 if axis == dim else 1 for axis in range(len(extent))])
    return gain


def setup_inputs(seed: int = 0) -> dict:
    streams_of = jax.random.split(jax.random.key(seed), 7)
    return {
        "sky_maps": draw_sky_maps(jax.random.fold_in(streams_of[6], 71), 0),
        "mode_vectors": draw_mode_vectors(jax.random.fold_in(streams_of[6], 71), 0),
        "pixel_weight": jnp.clip(jnp.exp(math.log(3.0) - 2.3025851 * jax.random.uniform(streams_of[2], (NPIX,), jnp.float32) ** steps_of(streams_of[2], (NPIX,), ((0, 32),), -0.2, 0.2)), 0.3, 3.0),
        "neighbours": draw_neighbours(jax.random.fold_in(streams_of[6], 71), 0),
        "tile_counts": draw_tile_counts(jax.random.fold_in(streams_of[6], 71), 0),
        "pair_bins": draw_pair_bins(jax.random.fold_in(streams_of[6], 71), 0),
    }


def orthonormal_basis(mode_vectors):
    columns = []
    for number in range(MODES):
        vector = mode_vectors[:, number]
        for earlier in columns:
            vector = vector - jnp.sum(earlier * vector) * earlier
        columns.append(vector / jnp.sqrt(jnp.sum(vector * vector) + 1e-06))
    return jnp.stack(columns, axis=1)

def projector(mode_vectors):
    basis = orthonormal_basis(mode_vectors)
    outer = jnp.dot(basis, basis.T, precision=lax.Precision.HIGHEST, preferred_element_type=jnp.float32)
    return jnp.eye(NCH, dtype=jnp.float32) - outer

def bin_masks(pair_bins):
    levels = jnp.arange(NBIN, dtype=jnp.int32)
    table = pair_bins[:, :, None, :] == levels[None, None, :, None]
    return table.astype(jnp.bfloat16).reshape(NBR, TILE, NBIN * TILE)

def taper_table():
    return 0.75 + 0.25 * jnp.cos(math.pi * jnp.arange(NBIN, dtype=jnp.float32) / NBIN)

def reference(sky_maps, mode_vectors, pixel_weight, neighbours, tile_counts, pair_bins):
    patch_count = NTB // TB
    chan_count = NTA // TA
    project = projector(mode_vectors)
    cleaned = jnp.dot(project, sky_maps, precision=lax.Precision.HIGHEST, preferred_element_type=jnp.float32)
    weighted = (cleaned * pixel_weight[None, :]).astype(jnp.bfloat16)
    stacked = jnp.concatenate([weighted, pixel_weight.astype(jnp.bfloat16)[None, :]], axis=0)
    grid_tiles = stacked.reshape(NCH + 1, patch_count, NTA, TB, TILE).transpose(0, 2, 1, 3, 4)
    grid_tiles = grid_tiles.reshape(NCH + 1, NTA, NTB, TILE)
    observed = tile_counts > 0
    core_maps = grid_tiles[:NCH].astype(jnp.float32)
    masked = jnp.where(observed[None, :, :, None], core_maps, jnp.float32(0.0))
    pixel_total = jnp.sum(observed.astype(jnp.float32)) * TILE
    covariance = jnp.einsum('cabq,dabq->cd', masked, core_maps, precision=lax.Precision.HIGHEST) / pixel_total
    mask_table = bin_masks(pair_bins).astype(jnp.float32)
    padded = jnp.pad(grid_tiles, ((0, 0), (1, 1), (1, 1), (0, 0)))
    zero_index = jnp.zeros((), jnp.int32)

    def region_sums(region):
        region = jnp.asarray(region).astype(jnp.int32)
        chan_block = (region // patch_count).astype(jnp.int32)
        patch_block = (region % patch_count).astype(jnp.int32)

        def tile_step(position, running):
            position = jnp.asarray(position).astype(jnp.int32)
            row_at = (chan_block * TA + position // TB).astype(jnp.int32)
            col_at = (patch_block * TB + position % TB).astype(jnp.int32)
            centre = lax.dynamic_slice(padded, (zero_index, (row_at + 1).astype(jnp.int32), (col_at + 1).astype(jnp.int32), zero_index), (NCH + 1, 1, 1, TILE))
            centre = centre.reshape(NCH + 1, TILE).astype(jnp.float32)

            def slot_step(slot_number, carried):
                slot_number = jnp.asarray(slot_number).astype(jnp.int32)
                offset_code = neighbours[row_at, col_at, slot_number].astype(jnp.int32)
                row_partner = (row_at + offset_code // 3).astype(jnp.int32)
                col_partner = (col_at + offset_code % 3).astype(jnp.int32)
                partner = lax.dynamic_slice(padded, (zero_index, row_partner, col_partner, zero_index), (NCH + 1, 1, 1, TILE))
                partner = partner.reshape(NCH + 1, TILE).astype(jnp.float32)
                binned = jnp.dot(centre, mask_table[offset_code], precision=lax.Precision.HIGHEST, preferred_element_type=jnp.float32)
                binned = binned.astype(jnp.bfloat16).astype(jnp.float32).reshape(NCH + 1, NBIN, TILE)
                return carried + jnp.einsum('cbr,dr->bcd', binned, partner, precision=lax.Precision.HIGHEST)
            slot_limit = tile_counts[row_at, col_at].astype(jnp.int32)
            return lax.fori_loop(jnp.int32(0), slot_limit, slot_step, running)
        start_sums = jnp.zeros((NBIN, NCH + 1, NCH + 1), jnp.float32)
        return lax.fori_loop(jnp.int32(0), jnp.int32(TA * TB), tile_step, start_sums)
    pair_sums = lax.map(region_sums, jnp.arange(chan_count * patch_count, dtype=jnp.int32))
    spread = jnp.sqrt(jnp.diagonal(covariance) + 1e-06)
    norm_scale = spread[:, None] * spread[None, :]
    pair_weight = jnp.maximum(pair_sums[:, :, NCH, NCH], 1.0)
    correlation = taper_table()[None, :, None, None] * pair_sums[:, :, :NCH, :NCH]
    correlation = correlation / (pair_weight[:, :, None, None] * norm_scale[None, None])
    return (correlation.reshape(chan_count, patch_count, NBIN, NCH, NCH), covariance)
```

```python
import functools
import math

import jax
import jax.numpy as jnp
from jax import lax
from jax.experimental import pallas as pl
from jax.experimental.pallas import tpu as pltpu
from jax.sharding import PartitionSpec as P

NCH = 64
MODES = 8
TILE = 128
NBIN = 8
NBR = 9
TA = 3
TB = 2
TILES = TA * TB
BLOCK = TILES * TILE
CORES = 2
F32 = jnp.float32
BF16 = jnp.bfloat16
HIGHEST = lax.Precision.HIGHEST
MESH = pl.DeviceIdType.MESH
NT = (((1,), (1,)), ((), ()))
SIDES = [(dk, dp) for dk in (-1, 0, 1) for dp in (-1, 0, 1) if (dk, dp) != (0, 0)]


def remote(src, dst, send, recv, chan, patch):
    return pltpu.make_async_remote_copy(
        src_ref=src,
        dst_ref=dst,
        send_sem=send,
        recv_sem=recv,
        device_id=(chan, patch),
        device_id_type=MESH,
    )


def span(step, extent):
    if step > 0:
        return pl.ds(extent, 1), pl.ds(0, 1)
    if step < 0:
        return pl.ds(1, 1), pl.ds(extent + 1, 1)
    return pl.ds(1, extent), pl.ds(1, extent)


def project_matrix(modes):
    lane = lax.broadcasted_iota(jnp.int32, (NCH, MODES), 1)
    for number in range(MODES):
        column = modes[:, number : number + 1]
        column = column / jnp.sqrt(jnp.sum(column * column, axis=0, keepdims=True) + 1e-06)
        inner = jnp.sum(modes * column, axis=0, keepdims=True)
        later = jnp.where(lane > number, modes - inner * column, modes)
        modes = jnp.where(lane == number, column, later)
    outer = lax.dot_general(modes, modes, NT, precision=HIGHEST, preferred_element_type=F32)
    return identity() - outer


def identity():
    rows = lax.broadcasted_iota(jnp.int32, (NCH, NCH), 0)
    cols = lax.broadcasted_iota(jnp.int32, (NCH, NCH), 1)
    return jnp.where(rows == cols, 1.0, 0.0).astype(F32)


def body(
    chans,
    patches,
    sky,
    modes,
    weight,
    nbr,
    cnt,
    bins,
    corr,
    cov_out,
    recv,
    w_own,
    w_left,
    w_right,
    table,
    mask,
    ext,
    cent,
    binned,
    w_binned,
    w_ext,
    w_part,
    acc,
    w_acc,
    piece,
    plane_in,
    z_out,
    z_in,
    whole_out,
    whole_in,
    packed_ref,
    local_sem,
    sky_send,
    sky_recv,
    w_send,
    w_recv,
    side_send,
    side_recv,
    plane_send,
    plane_recv,
    z_send,
    z_recv,
    whole_send,
    whole_recv,
):
    depth = patches // CORES
    plane = chans * CORES
    chan = lax.axis_index("chan")
    patch = lax.axis_index("patch")
    z = patch // CORES
    core = patch % CORES
    seat = chan * CORES + core

    def seat_device(other):
        return other // CORES, z * CORES + other % CORES

    def z_device(other):
        return chan, other * CORES + core

    table_copy = pltpu.make_async_copy(bins, table, local_sem.at[0])
    table_copy.start()
    weight_copy = pltpu.make_async_copy(weight, w_own, local_sem.at[1])
    weight_copy.start()

    def columns(other):
        return sky.at[:, pl.ds(pl.multiple_of(other * BLOCK, BLOCK), BLOCK)]

    own_copy = pltpu.make_async_copy(columns(chan), recv.at[chan], local_sem.at[2])
    own_copy.start()

    barrier = pltpu.get_barrier_semaphore()

    def greet(c, p):
        pl.semaphore_signal(barrier, inc=1, device_id=(c, p), device_id_type=MESH)

    @pl.loop(1, depth)
    def _(step):
        greet(*z_device((z + step) % depth))

    far = (patch + 2 * core - 1 + patches) % patches
    for shift in range(3):
        greet((chan + shift - 1 + chans) % chans, far)

    @pl.loop(1, plane)
    def _(step):
        greet(*seat_device((seat + step) % plane))

    pl.semaphore_wait(barrier, depth - 1 + 3 + plane - 1)

    def sky_copy(step):
        other = (chan + step) % chans
        return remote(
            columns(other), recv.at[chan], sky_send.at[step], sky_recv.at[step], other, patch
        )

    @pl.loop(1, chans)
    def _(step):
        sky_copy(step).start()

    right = (patch + 1) % patches
    left = (patch + patches - 1) % patches
    to_right = remote(weight, w_left, w_send.at[0], w_recv.at[0], chan, right)
    to_left = remote(weight, w_right, w_send.at[1], w_recv.at[1], chan, left)
    to_right.start()
    to_left.start()

    project = project_matrix(modes[...])

    table_copy.wait()

    @pl.loop(0, NBR)
    def _(code):
        bins_here = table[code]
        for level in range(NBIN):
            mask[code, :, level * TILE : (level + 1) * TILE] = jnp.where(
                bins_here == level, 1.0, 0.0
            ).astype(BF16)

    bits = []
    seen = []
    for a in range(TA):
        for b in range(TB):
            count = cnt[a, b]
            flags = jnp.int32(0)
            for slot in range(NBR):
                flags = flags + jnp.where(slot < count, jnp.int32(1) << nbr[a, b, slot], 0)
            bits.append(flags)
            seen.append(jnp.where(count > 0, 1.0, 0.0).astype(F32))

    weight_copy.wait()
    to_right.wait()
    to_left.wait()
    for row in range(TA + 2):
        tile_row = jnp.clip(chan * TA + row - 1, 0, chans * TA - 1)
        for col, (source, side) in enumerate(
            ((w_left, 1), (w_own, 0), (w_own, 1), (w_right, 0))
        ):
            w_ext[col, row] = source[tile_row * TB + side].astype(BF16).astype(F32)
    w_part[...] = jnp.zeros_like(w_part)
    for t in range(TILES):
        w_part[t : t + 1, :] = w_ext[1 + t % TB, 1 + t // TB]
    cent[TILES * NCH :, :] = w_part[...].astype(BF16)
    w_line = jnp.concatenate([w_own[chan * TILES + t] for t in range(TILES)], axis=1)
    acc[...] = jnp.zeros_like(acc)
    w_acc[...] = jnp.zeros_like(w_acc)

    own_copy.wait()

    @pl.loop(1, chans)
    def _(step):
        other = (chan + chans - step) % chans
        sky_copy(step).wait_send()
        remote(
            recv.at[other], recv.at[other], sky_send.at[step], sky_recv.at[step], other, patch
        ).wait_recv()

    gathered = recv[...].reshape(NCH, BLOCK)
    cleaned = lax.dot_general(
        project,
        gathered,
        (((1,), (0,)), ((), ())),
        precision=HIGHEST,
        preferred_element_type=F32,
    )
    weighted32 = cleaned * w_line
    weighted = weighted32.astype(BF16)
    for t in range(TILES):
        tile = weighted[:, t * TILE : (t + 1) * TILE]
        ext[1 + t % TB, 1 + t // TB] = tile
        cent[t * NCH : (t + 1) * NCH, :] = tile

    side_copies = []
    for number, (dk, dp) in enumerate(SIDES):
        row_src, row_dst = span(dk, TA)
        col_src, col_dst = span(dp, TB)
        copy = remote(
            ext.at[col_src, row_src],
            ext.at[col_dst, row_dst],
            side_send.at[number],
            side_recv.at[number],
            (chan + dk + chans) % chans,
            (patch + dp + patches) % patches,
        )
        copy.start()
        side_copies.append(copy)

    masked = jnp.concatenate(
        [
            (cent[t * NCH : (t + 1) * NCH, :].astype(F32) * seen[t]).astype(BF16)
            for t in range(TILES)
        ],
        axis=1,
    )
    part = lax.dot_general(masked, weighted, NT, preferred_element_type=F32)
    half = NCH // 2
    packed = jnp.concatenate([part[:half], part[half:]], axis=1)
    total = functools.reduce(lambda x, y: x + y, seen) * TILE
    for row in range(half):
        piece[row, 0:1, :] = packed[row : row + 1, :]
    piece[:, 1:2, :] = jnp.full((half, 1, TILE), total, F32)

    def plane_copy(step):
        other = (seat + step) % plane
        return remote(
            piece.at[other],
            plane_in.at[seat],
            plane_send.at[step],
            plane_recv.at[step],
            *seat_device(other),
        )

    @pl.loop(1, plane)
    def _(step):
        plane_copy(step).start()

    plane_in[seat] = piece[seat]

    @pl.loop(0, NBR)
    def _(code):
        centres = cent[...]
        for pair in range(NBIN // 2):
            lanes = slice(2 * pair * TILE, 2 * (pair + 1) * TILE)
            sums = jnp.dot(centres, mask[code, :, lanes], preferred_element_type=F32).astype(BF16)
            for half_bin in range(2):
                level = 2 * pair + half_bin
                cut = sums[:, half_bin * TILE : (half_bin + 1) * TILE]
                for t in range(TILES):
                    binned[
                        code,
                        level * NCH : (level + 1) * NCH,
                        t * TILE : (t + 1) * TILE,
                    ] = cut[t * NCH : (t + 1) * NCH, :]
                w_binned[code, :, level * TILE : (level + 1) * TILE] = cut[TILES * NCH :, :]

    @pl.loop(1, plane)
    def _(step):
        other = (seat + plane - step) % plane
        plane_copy(step).wait_send()
        remote(
            plane_in.at[other],
            plane_in.at[other],
            plane_send.at[step],
            plane_recv.at[step],
            *seat_device(other),
        ).wait_recv()

    plane_sum = jnp.sum(plane_in[...], axis=0)
    z_out[...] = plane_sum
    z_in[z] = plane_sum

    def z_copy(step):
        return remote(
            z_out, z_in.at[z], z_send.at[step], z_recv.at[step], *z_device((z + step) % depth)
        )

    @pl.loop(1, depth)
    def _(step):
        z_copy(step).start()

    for copy in side_copies:
        copy.wait()

    @pl.loop(0, NBR)
    def _(code):
        row_shift = code // 3
        col_shift = code % 3
        parts = []
        for t in range(TILES):
            present = ((bits[t] >> code) & 1).astype(F32)
            tile = ext[t % TB + col_shift, t // TB + row_shift]
            parts.append((tile.astype(F32) * present).astype(BF16))
            w_part[t : t + 1, :] = w_ext[t % TB + col_shift, t // TB + row_shift] * present
        partners = jnp.concatenate(parts, axis=1)
        acc[...] += lax.dot_general(binned[code], partners, NT, preferred_element_type=F32)
        w_tiles = w_part[0:8, :]
        w_acc[...] += w_binned[code].astype(F32)[0:8, :] * jnp.concatenate(
            [w_tiles] * NBIN, axis=1
        )

    @pl.loop(1, depth)
    def _(step):
        other = (z + depth - step) % depth
        z_copy(step).wait_send()
        remote(
            z_in.at[other], z_in.at[other], z_send.at[step], z_recv.at[step], *z_device(other)
        ).wait_recv()

    z_sum = jnp.sum(z_in[...], axis=0)
    whole_out[...] = z_sum
    whole_in[seat] = z_sum

    def whole_copy(step):
        return remote(
            whole_out,
            whole_in.at[seat],
            whole_send.at[step],
            whole_recv.at[step],
            *seat_device((seat + step) % plane),
        )

    @pl.loop(1, plane)
    def _(step):
        whole_copy(step).start()

    @pl.loop(1, plane)
    def _(step):
        other = (seat + plane - step) % plane
        whole_copy(step).wait_send()
        remote(
            whole_in.at[other],
            whole_in.at[other],
            whole_send.at[step],
            whole_recv.at[step],
            *seat_device(other),
        ).wait_recv()

    for row in range(half):
        packed_ref[row : row + 1, :] = whole_in[row, 0:1, :] / whole_in[row, 1:2, :]
    lines = packed_ref[...]
    covariance = jnp.concatenate([lines[:, :NCH], lines[:, NCH:]], axis=0)
    cov_out[...] = covariance
    only = covariance * identity()
    down = jnp.sqrt(jnp.sum(only, axis=1, keepdims=True) + 1e-06)
    across = jnp.sqrt(jnp.sum(only, axis=0, keepdims=True) + 1e-06)
    norm = down * across
    for level in range(NBIN):
        chunk = w_acc[:, level * TILE : (level + 1) * TILE]
        pairs = jnp.sum(jnp.sum(chunk, axis=0, keepdims=True), axis=1, keepdims=True)
        taper = 0.75 + 0.25 * math.cos(math.pi * level / NBIN)
        rows = acc[level * NCH : (level + 1) * NCH, :]
        corr[level] = taper * rows / (jnp.maximum(pairs, 1.0) * norm)


def per_device(sky_maps, mode_vectors, pixel_weight, neighbours, tile_counts, pair_bins):
    chans = lax.axis_size("chan")
    patches = lax.axis_size("patch")
    plane = chans * CORES
    depth = patches // CORES
    rows = chans * TILES
    weight = pixel_weight.reshape(rows, 1, TILE)
    dma = pltpu.SemaphoreType.DMA
    vmem = pltpu.VMEM
    anywhere = pl.BlockSpec(memory_space=pl.ANY)
    in_vmem = pl.BlockSpec(memory_space=pltpu.VMEM)
    in_smem = pl.BlockSpec(memory_space=pltpu.SMEM)
    correlation, covariance = pl.pallas_call(
        functools.partial(body, chans, patches),
        out_shape=(
            jax.ShapeDtypeStruct((NBIN, NCH, NCH), F32),
            jax.ShapeDtypeStruct((NCH, NCH), F32),
        ),
        in_specs=[anywhere, in_vmem, anywhere, in_smem, in_smem, anywhere],
        out_specs=(in_vmem, in_vmem),
        scratch_shapes=[
            vmem((chans, NCH // chans, BLOCK), F32),
            vmem((rows, 1, TILE), F32),
            vmem((rows, 1, TILE), F32),
            vmem((rows, 1, TILE), F32),
            vmem((NBR, TILE, TILE), jnp.int32),
            vmem((NBR, TILE, NBIN * TILE), BF16),
            vmem((TB + 2, TA + 2, NCH, TILE), BF16),
            vmem((TILES * NCH + 16, TILE), BF16),
            vmem((NBR, NBIN * NCH, BLOCK), BF16),
            vmem((NBR, 16, NBIN * TILE), BF16),
            vmem((TB + 2, TA + 2, 1, TILE), F32),
            vmem((16, TILE), F32),
            vmem((NBIN * NCH, NCH), F32),
            vmem((8, NBIN * TILE), F32),
            vmem((plane, 2, TILE), F32),
            vmem((plane, 2, TILE), F32),
            vmem((2, TILE), F32),
            vmem((depth, 2, TILE), F32),
            vmem((2, TILE), F32),
            vmem((plane, 2, TILE), F32),
            vmem((NCH // 2, TILE), F32),
            dma((3,)),
            dma((chans,)),
            dma((chans,)),
            dma((2,)),
            dma((2,)),
            dma((len(SIDES),)),
            dma((len(SIDES),)),
            dma((plane,)),
            dma((plane,)),
            dma((depth,)),
            dma((depth,)),
            dma((plane,)),
            dma((plane,)),
        ],
        compiler_params=pltpu.CompilerParams(collective_id=0, has_side_effects=True),
        name="sky_pairs",
    )(sky_maps, mode_vectors, weight, neighbours, tile_counts, pair_bins)
    return (correlation[None, None], covariance)


def solution(mesh):
    return jax.shard_map(
        per_device,
        mesh=mesh,
        in_specs=(
            P("chan", "patch"),
            P(),
            P("patch"),
            P("chan", "patch", None),
            P("chan", "patch"),
            P(),
        ),
        out_specs=(P("chan", "patch", None, None, None), P()),
        check_vma=False,
    )
```

```python
import functools
import math

import jax
import jax.numpy as jnp
from jax import lax
from jax.experimental import pallas as pl
from jax.experimental.pallas import tpu as pltpu
from jax.sharding import PartitionSpec as P

NCH = 64
MODES = 8
TILE = 128
NBIN = 8
NBR = 9
TA = 3
TB = 2
TILES = TA * TB
BLOCK = TILES * TILE
CORES = 2
F32 = jnp.float32
BF16 = jnp.bfloat16
HIGHEST = lax.Precision.HIGHEST
MESH = pl.DeviceIdType.MESH
NT = (((1,), (1,)), ((), ()))
SIDES = [(dk, dp) for dk in (-1, 0, 1) for dp in (-1, 0, 1) if (dk, dp) != (0, 0)]


def remote(src, dst, send, recv, chan, patch):
    return pltpu.make_async_remote_copy(
        src_ref=src,
        dst_ref=dst,
        send_sem=send,
        recv_sem=recv,
        device_id=(chan, patch),
        device_id_type=MESH,
    )


def span(step, extent):
    if step > 0:
        return pl.ds(extent, 1), pl.ds(0, 1)
    if step < 0:
        return pl.ds(1, 1), pl.ds(extent + 1, 1)
    return pl.ds(1, extent), pl.ds(1, extent)


def project_matrix(modes):
    lane = lax.broadcasted_iota(jnp.int32, (NCH, MODES), 1)
    for number in range(MODES):
        column = modes[:, number : number + 1]
        column = column / jnp.sqrt(jnp.sum(column * column, axis=0, keepdims=True) + 1e-06)
        inner = jnp.sum(modes * column, axis=0, keepdims=True)
        later = jnp.where(lane > number, modes - inner * column, modes)
        modes = jnp.where(lane == number, column, later)
    outer = lax.dot_general(modes, modes, NT, precision=HIGHEST, preferred_element_type=F32)
    return identity() - outer


def identity():
    rows = lax.broadcasted_iota(jnp.int32, (NCH, NCH), 0)
    cols = lax.broadcasted_iota(jnp.int32, (NCH, NCH), 1)
    return jnp.where(rows == cols, 1.0, 0.0).astype(F32)


def body(
    chans,
    patches,
    sky,
    modes,
    weight,
    nbr,
    cnt,
    bins,
    corr,
    cov_out,
    recv,
    modes_in,
    nbr_in,
    cnt_in,
    present,
    seen,
    w_own,
    w_left,
    w_right,
    table,
    mask,
    ext,
    cent,
    binned,
    w_binned,
    w_ext,
    w_part,
    acc,
    w_acc,
    piece,
    plane_in,
    z_out,
    z_in,
    whole_out,
    whole_in,
    packed_ref,
    local_sem,
    sky_send,
    sky_recv,
    w_send,
    w_recv,
    side_send,
    side_recv,
    plane_send,
    plane_recv,
    z_send,
    z_recv,
    whole_send,
    whole_recv,
    ready,
):
    depth = patches // CORES
    plane = chans * CORES
    side = math.isqrt(chans)
    chan = lax.axis_index("chan")
    patch = lax.axis_index("patch")
    z = patch // CORES
    core = patch % CORES
    seat = chan * CORES + core
    chan_y = chan // side
    chan_x = chan % side

    shifts = [(dy, dx) for dy in range(side) for dx in range(side)]
    shifts.sort(key=lambda d: -(min(d[0], side - d[0]) + min(d[1], side - d[1])))
    ahead = [(chan_y + dy) % side * side + (chan_x + dx) % side for dy, dx in shifts]
    behind = [
        (chan_y + side - dy) % side * side + (chan_x + side - dx) % side for dy, dx in shifts
    ]
    cores = (core, 1 - core)
    seats = [(i, c) for i in range(chans) for c in range(CORES) if (i, c) != (chans - 1, 0)]

    def z_device(other):
        return chan, other * CORES + core

    def signal(semaphore, device):
        pl.semaphore_signal(semaphore, inc=1, device_id=device, device_id_type=MESH)

    barrier = pltpu.get_barrier_semaphore()
    far = (patch + 2 * core - 1 + patches) % patches
    for shift in range(3):
        signal(barrier, ((chan + shift - 1 + chans) % chans, far))
    for i, c in seats:
        signal(barrier, (ahead[i], z * CORES + cores[c]))
    signal(barrier, z_device((z + 1) % depth))
    signal(barrier, z_device((z + depth - 1) % depth))

    def columns(other):
        return sky.at[:, pl.ds(pl.multiple_of(other * BLOCK, BLOCK), BLOCK)]

    local_copies = [
        pltpu.make_async_copy(source, target, local_sem.at[number])
        for number, (source, target) in enumerate(
            (
                (modes, modes_in),
                (bins, table),
                (nbr, nbr_in),
                (cnt, cnt_in),
                (weight, w_own),
                (columns(chan), recv.at[chan]),
            )
        )
    ]
    for copy in local_copies:
        copy.start()

    pl.semaphore_wait(barrier, 3 + len(seats) + 2)

    def sky_copy(i):
        return remote(
            columns(ahead[i]), recv.at[chan], sky_send.at[i], sky_recv.at[i], ahead[i], patch
        )

    for i in range(chans - 1):
        sky_copy(i).start()

    right = (patch + 1) % patches
    left = (patch + patches - 1) % patches
    to_right = remote(weight, w_left, w_send.at[0], w_recv.at[0], chan, right)
    to_left = remote(weight, w_right, w_send.at[1], w_recv.at[1], chan, left)
    to_right.start()
    to_left.start()

    reaches = [1 << r for r in range((depth // 2).bit_length() - 1)]

    def announce(r):
        signal(ready.at[r], z_device((z + reaches[r]) % depth))
        signal(ready.at[r], z_device((z + depth - reaches[r]) % depth))

    def hear(r):
        pl.semaphore_wait(ready.at[r], 2)

    announce(0)
    for copy in local_copies[:-1]:
        copy.wait()

    project = project_matrix(modes_in[...].T)
    hear(0)
    announce(1)

    @pl.loop(0, NBR)
    def _(code):
        bins_here = table[code]
        for level in range(NBIN):
            mask[code, :, level * TILE : (level + 1) * TILE] = jnp.where(
                bins_here == level, 1.0, 0.0
            ).astype(BF16)

    slots = lax.broadcasted_iota(jnp.int32, (TB, NBR), 1)
    for a in range(TA):
        count = cnt_in[:, a : a + 1]
        live = jnp.where(slots < count, nbr_in[a], NBR)
        observed = jnp.broadcast_to(jnp.where(count > 0, 1.0, 0.0).astype(F32), (TB, TILE))
        for b in range(TB):
            seen[a * TB + b] = observed[b : b + 1, :]
        for code in range(NBR):
            hit = jnp.max(jnp.where(live == code, 1.0, 0.0).astype(F32), axis=1, keepdims=True)
            hit = jnp.broadcast_to(hit, (TB, TILE))
            for b in range(TB):
                present[code, a * TB + b] = hit[b : b + 1, :]
    for r in range(1, len(reaches) - 1):
        hear(r)
        announce(r + 1)

    to_right.wait()
    to_left.wait()
    for row in range(TA + 2):
        tile_row = jnp.clip(chan * TA + row - 1, 0, chans * TA - 1)
        for col, (source, side) in enumerate(
            ((w_left, 1), (w_own, 0), (w_own, 1), (w_right, 0))
        ):
            w_ext[col, row] = source[tile_row * TB + side].astype(BF16).astype(F32)
    w_part[...] = jnp.zeros_like(w_part)
    for t in range(TILES):
        w_part[t : t + 1, :] = w_ext[1 + t % TB, 1 + t // TB]
    cent[TILES * NCH :, :] = w_part[...].astype(BF16)
    w_line = jnp.concatenate([w_own[chan * TILES + t] for t in range(TILES)], axis=1)
    acc[...] = jnp.zeros_like(acc)
    w_acc[...] = jnp.zeros_like(w_acc)

    local_copies[-1].wait()
    for i in range(chans - 1):
        sky_copy(i).wait_send()
        remote(
            recv.at[behind[i]],
            recv.at[behind[i]],
            sky_send.at[i],
            sky_recv.at[i],
            behind[i],
            patch,
        ).wait_recv()

    gathered = recv[...].reshape(NCH, BLOCK)
    cleaned = lax.dot_general(
        project,
        gathered,
        (((1,), (0,)), ((), ())),
        precision=HIGHEST,
        preferred_element_type=F32,
    )
    weighted32 = cleaned * w_line
    weighted = weighted32.astype(BF16)
    for t in range(TILES):
        tile = weighted[:, t * TILE : (t + 1) * TILE]
        ext[1 + t % TB, 1 + t // TB] = tile
        cent[t * NCH : (t + 1) * NCH, :] = tile

    side_copies = []
    for number, (dk, dp) in enumerate(SIDES):
        row_src, row_dst = span(dk, TA)
        col_src, col_dst = span(dp, TB)
        copy = remote(
            ext.at[col_src, row_src],
            ext.at[col_dst, row_dst],
            side_send.at[number],
            side_recv.at[number],
            (chan + dk + chans) % chans,
            (patch + dp + patches) % patches,
        )
        copy.start()
        side_copies.append(copy)

    masked = jnp.concatenate(
        [
            (cent[t * NCH : (t + 1) * NCH, :].astype(F32) * seen[t]).astype(BF16)
            for t in range(TILES)
        ],
        axis=1,
    )
    part = lax.dot_general(masked, weighted, NT, preferred_element_type=F32)
    half = NCH // 2
    packed = jnp.concatenate([part[:half], part[half:]], axis=1)
    total = jnp.sum(seen[...], axis=0) * TILE
    for row in range(half):
        piece[row, 0:1, :] = packed[row : row + 1, :]
    piece[:, 1:2, :] = jnp.broadcast_to(total[None], (half, 1, TILE))

    def seat_of(chan_list, n):
        i, c = seats[n]
        return chan_list[i] * CORES + cores[c]

    def plane_start(n, source, target, send, recv_sem):
        i, c = seats[n]
        copy = remote(
            source, target, send.at[n], recv_sem.at[n], ahead[i], z * CORES + cores[c]
        )
        copy.start()
        return copy

    def plane_wait(n, sent, target, send, recv_sem):
        i, c = seats[n]
        slot = target.at[seat_of(behind, n)]
        sent.wait_send()
        remote(
            slot, slot, send.at[n], recv_sem.at[n], behind[i], z * CORES + cores[c]
        ).wait_recv()

    plane_copies = [
        plane_start(n, piece.at[seat_of(ahead, n)], plane_in.at[seat], plane_send, plane_recv)
        for n in range(len(seats))
    ]

    plane_in[seat] = piece[seat]

    @pl.loop(0, NBR)
    def _(code):
        centres = cent[...]
        for pair in range(NBIN // 2):
            lanes = slice(2 * pair * TILE, 2 * (pair + 1) * TILE)
            sums = jnp.dot(centres, mask[code, :, lanes], preferred_element_type=F32).astype(BF16)
            for half_bin in range(2):
                level = 2 * pair + half_bin
                cut = sums[:, half_bin * TILE : (half_bin + 1) * TILE]
                for t in range(TILES):
                    binned[
                        code,
                        level * NCH : (level + 1) * NCH,
                        t * TILE : (t + 1) * TILE,
                    ] = cut[t * NCH : (t + 1) * NCH, :]
                w_binned[code, :, level * TILE : (level + 1) * TILE] = cut[TILES * NCH :, :]

    for n in range(len(seats)):
        plane_wait(n, plane_copies[n], plane_in, plane_send, plane_recv)

    plane_sum = jnp.sum(plane_in[...], axis=0)
    z_out[...] = plane_sum
    z_in[z] = plane_sum

    def z_copy(step):
        return remote(
            z_out, z_in.at[z], z_send.at[step], z_recv.at[step], *z_device((z + step) % depth)
        )

    hear(len(reaches) - 1)

    @pl.loop(1, depth)
    def _(step):
        z_copy(step).start()

    for copy in side_copies:
        copy.wait()

    @pl.loop(0, NBR)
    def _(code):
        row_shift = code // 3
        col_shift = code % 3
        parts = []
        for t in range(TILES):
            here = present[code, t]
            tile = ext[t % TB + col_shift, t // TB + row_shift]
            parts.append((tile.astype(F32) * here).astype(BF16))
            w_part[t : t + 1, :] = w_ext[t % TB + col_shift, t // TB + row_shift] * here
        partners = jnp.concatenate(parts, axis=1)
        acc[...] += lax.dot_general(binned[code], partners, NT, preferred_element_type=F32)
        w_tiles = w_part[0:8, :]
        w_acc[...] += w_binned[code].astype(F32)[0:8, :] * jnp.concatenate(
            [w_tiles] * NBIN, axis=1
        )

    @pl.loop(1, depth)
    def _(step):
        other = (z + depth - step) % depth
        z_copy(step).wait_send()
        remote(
            z_in.at[other], z_in.at[other], z_send.at[step], z_recv.at[step], *z_device(other)
        ).wait_recv()

    z_sum = jnp.sum(z_in[...], axis=0)
    whole_out[...] = z_sum
    whole_in[seat] = z_sum

    whole_copies = [
        plane_start(n, whole_out, whole_in.at[seat], whole_send, whole_recv)
        for n in range(len(seats))
    ]
    scales = []
    for level in range(NBIN):
        chunk = w_acc[:, level * TILE : (level + 1) * TILE]
        scales.append(
            jnp.maximum(jnp.sum(jnp.sum(chunk, axis=0, keepdims=True), axis=1, keepdims=True), 1.0)
        )
    for n in range(len(seats)):
        plane_wait(n, whole_copies[n], whole_in, whole_send, whole_recv)

    for row in range(half):
        packed_ref[row : row + 1, :] = whole_in[row, 0:1, :] / whole_in[row, 1:2, :]
    lines = packed_ref[...]
    covariance = jnp.concatenate([lines[:, :NCH], lines[:, NCH:]], axis=0)
    cov_out[...] = covariance
    only = covariance * identity()
    down = jnp.sqrt(jnp.sum(only, axis=1, keepdims=True) + 1e-06)
    across = jnp.sqrt(jnp.sum(only, axis=0, keepdims=True) + 1e-06)
    norm = down * across
    for level in range(NBIN):
        taper = 0.75 + 0.25 * math.cos(math.pi * level / NBIN)
        rows = acc[level * NCH : (level + 1) * NCH, :]
        corr[level] = taper * rows / (scales[level] * norm)


def per_device(sky_maps, mode_vectors, pixel_weight, neighbours, tile_counts, pair_bins):
    chans = lax.axis_size("chan")
    patches = lax.axis_size("patch")
    plane = chans * CORES
    depth = patches // CORES
    rows = chans * TILES
    weight = pixel_weight.reshape(rows, 1, TILE)
    dma = pltpu.SemaphoreType.DMA
    vmem = pltpu.VMEM
    anywhere = pl.BlockSpec(memory_space=pl.ANY)
    in_vmem = pl.BlockSpec(memory_space=pltpu.VMEM)
    correlation, covariance = pl.pallas_call(
        functools.partial(body, chans, patches),
        out_shape=(
            jax.ShapeDtypeStruct((NBIN, NCH, NCH), F32),
            jax.ShapeDtypeStruct((NCH, NCH), F32),
        ),
        in_specs=[anywhere] * 6,
        out_specs=(in_vmem, in_vmem),
        scratch_shapes=[
            vmem((chans, NCH // chans, BLOCK), F32),
            vmem((MODES, NCH), F32),
            vmem((TA, TB, NBR), jnp.int32),
            vmem((TB, TA), jnp.int32),
            vmem((NBR, TILES, 1, TILE), F32),
            vmem((TILES, 1, TILE), F32),
            vmem((rows, 1, TILE), F32),
            vmem((rows, 1, TILE), F32),
            vmem((rows, 1, TILE), F32),
            vmem((NBR, TILE, TILE), jnp.int32),
            vmem((NBR, TILE, NBIN * TILE), BF16),
            vmem((TB + 2, TA + 2, NCH, TILE), BF16),
            vmem((TILES * NCH + 16, TILE), BF16),
            vmem((NBR, NBIN * NCH, BLOCK), BF16),
            vmem((NBR, 16, NBIN * TILE), BF16),
            vmem((TB + 2, TA + 2, 1, TILE), F32),
            vmem((16, TILE), F32),
            vmem((NBIN * NCH, NCH), F32),
            vmem((8, NBIN * TILE), F32),
            vmem((plane, 2, TILE), F32),
            vmem((plane, 2, TILE), F32),
            vmem((2, TILE), F32),
            vmem((depth, 2, TILE), F32),
            vmem((2, TILE), F32),
            vmem((plane, 2, TILE), F32),
            vmem((NCH // 2, TILE), F32),
            dma((6,)),
            dma((chans,)),
            dma((chans,)),
            dma((2,)),
            dma((2,)),
            dma((len(SIDES),)),
            dma((len(SIDES),)),
            dma((plane,)),
            dma((plane,)),
            dma((depth,)),
            dma((depth,)),
            dma((plane,)),
            dma((plane,)),
            pltpu.SemaphoreType.REGULAR((max(1, (depth // 2).bit_length() - 1),)),
        ],
        compiler_params=pltpu.CompilerParams(collective_id=0, has_side_effects=True),
        name="sky_pairs",
    )(sky_maps, mode_vectors.T, weight, neighbours, tile_counts.T, pair_bins)
    return (correlation[None, None], covariance)


def solution(mesh):
    return jax.shard_map(
        per_device,
        mesh=mesh,
        in_specs=(
            P("chan", "patch"),
            P(),
            P("patch"),
            P("chan", "patch", None),
            P("chan", "patch"),
            P(),
        ),
        out_specs=(P("chan", "patch", None, None, None), P()),
        check_vma=False,
    )
```

```python
import functools
import math

import jax
import jax.numpy as jnp
from jax import lax
from jax.experimental import pallas as pl
from jax.experimental.pallas import tpu as pltpu
from jax.sharding import PartitionSpec as P

NCH = 64
MODES = 8
TILE = 128
NBIN = 8
NBR = 9
TA = 3
TB = 2
TILES = TA * TB
BLOCK = TILES * TILE
CORES = 2
F32 = jnp.float32
BF16 = jnp.bfloat16
HIGHEST = lax.Precision.HIGHEST
MESH = pl.DeviceIdType.MESH
NT = (((1,), (1,)), ((), ()))
SIDES = [(dk, dp) for dk in (-1, 0, 1) for dp in (-1, 0, 1) if (dk, dp) != (0, 0)]


def remote(src, dst, send, recv, chan, patch):
    return pltpu.make_async_remote_copy(
        src_ref=src,
        dst_ref=dst,
        send_sem=send,
        recv_sem=recv,
        device_id=(chan, patch),
        device_id_type=MESH,
    )


def span(step, extent):
    if step > 0:
        return pl.ds(extent, 1), pl.ds(0, 1)
    if step < 0:
        return pl.ds(1, 1), pl.ds(extent + 1, 1)
    return pl.ds(1, extent), pl.ds(1, extent)


def project_matrix(modes):
    lane = lax.broadcasted_iota(jnp.int32, (NCH, MODES), 1)
    for number in range(MODES):
        column = modes[:, number : number + 1]
        column = column / jnp.sqrt(jnp.sum(column * column, axis=0, keepdims=True) + 1e-06)
        inner = jnp.sum(modes * column, axis=0, keepdims=True)
        later = jnp.where(lane > number, modes - inner * column, modes)
        modes = jnp.where(lane == number, column, later)
    outer = lax.dot_general(modes, modes, NT, precision=HIGHEST, preferred_element_type=F32)
    return identity() - outer


def identity():
    rows = lax.broadcasted_iota(jnp.int32, (NCH, NCH), 0)
    cols = lax.broadcasted_iota(jnp.int32, (NCH, NCH), 1)
    return jnp.where(rows == cols, 1.0, 0.0).astype(F32)


def body(
    chans,
    patches,
    sky,
    modes,
    weight,
    nbr,
    cnt,
    bins,
    corr,
    cov_out,
    recv,
    sky_in,
    modes_in,
    nbr_in,
    cnt_in,
    present,
    seen,
    w_own,
    w_left,
    w_right,
    table,
    mask,
    ext,
    cent,
    binned,
    w_binned,
    w_ext,
    w_part,
    acc,
    w_acc,
    piece,
    plane_in,
    z_out,
    z_in,
    whole_out,
    whole_in,
    packed_ref,
    local_sem,
    sky_send,
    sky_recv,
    w_send,
    w_recv,
    side_send,
    side_recv,
    plane_send,
    plane_recv,
    z_send,
    z_recv,
    whole_send,
    whole_recv,
    ready,
):
    depth = patches // CORES
    plane = chans * CORES
    side = math.isqrt(chans)
    chan = lax.axis_index("chan")
    patch = lax.axis_index("patch")
    z = patch // CORES
    core = patch % CORES
    seat = chan * CORES + core
    chan_y = chan // side
    chan_x = chan % side

    shifts = [(dy, dx) for dy in range(side) for dx in range(side)]
    shifts.sort(key=lambda d: -(min(d[0], side - d[0]) + min(d[1], side - d[1])))
    ahead = [(chan_y + dy) % side * side + (chan_x + dx) % side for dy, dx in shifts]
    behind = [
        (chan_y + side - dy) % side * side + (chan_x + side - dx) % side for dy, dx in shifts
    ]
    cores = (core, 1 - core)
    seats = [(i, c) for i in range(chans) for c in range(CORES) if (i, c) != (chans - 1, 0)]

    def z_device(other):
        return chan, other * CORES + core

    def signal(semaphore, device):
        pl.semaphore_signal(semaphore, inc=1, device_id=device, device_id_type=MESH)

    barrier = pltpu.get_barrier_semaphore()
    far = (patch + 2 * core - 1 + patches) % patches
    for shift in range(3):
        signal(barrier, ((chan + shift - 1 + chans) % chans, far))
    for i, c in seats:
        signal(barrier, (ahead[i], z * CORES + cores[c]))
    signal(barrier, z_device((z + 1) % depth))
    signal(barrier, z_device((z + depth - 1) % depth))

    def columns(other):
        return sky_in.at[:, pl.ds(pl.multiple_of(other * BLOCK, BLOCK), BLOCK)]

    local_copies = [
        pltpu.make_async_copy(source, target, local_sem.at[number])
        for number, (source, target) in enumerate(
            (
                (modes, modes_in),
                (bins, table),
                (nbr, nbr_in),
                (cnt, cnt_in),
                (weight, w_own),
                (sky, sky_in),
            )
        )
    ]
    for copy in local_copies:
        copy.start()

    local_copies[-1].wait()
    pl.semaphore_wait(barrier, 3 + len(seats) + 2)

    def sky_copy(i):
        return remote(
            columns(ahead[i]), recv.at[chan], sky_send.at[i], sky_recv.at[i], ahead[i], patch
        )

    for i in range(chans - 1):
        sky_copy(i).start()

    right = (patch + 1) % patches
    left = (patch + patches - 1) % patches
    to_right = remote(weight, w_left, w_send.at[0], w_recv.at[0], chan, right)
    to_left = remote(weight, w_right, w_send.at[1], w_recv.at[1], chan, left)
    to_right.start()
    to_left.start()

    reaches = [1 << r for r in range((depth // 2).bit_length() - 1)]

    def announce(r):
        signal(ready.at[r], z_device((z + reaches[r]) % depth))
        signal(ready.at[r], z_device((z + depth - reaches[r]) % depth))

    def hear(r):
        pl.semaphore_wait(ready.at[r], 2)

    announce(0)
    recv[chan] = sky_in[:, pl.ds(pl.multiple_of(chan * BLOCK, BLOCK), BLOCK)]
    for copy in local_copies[:-1]:
        copy.wait()

    project = project_matrix(modes_in[...].T)
    hear(0)
    announce(1)

    @pl.loop(0, NBR)
    def _(code):
        bins_here = table[code]
        for level in range(NBIN):
            mask[code, :, level * TILE : (level + 1) * TILE] = jnp.where(
                bins_here == level, 1.0, 0.0
            ).astype(BF16)

    slots = lax.broadcasted_iota(jnp.int32, (TB, NBR), 1)
    for a in range(TA):
        count = cnt_in[:, a : a + 1]
        live = jnp.where(slots < count, nbr_in[a], NBR)
        observed = jnp.broadcast_to(jnp.where(count > 0, 1.0, 0.0).astype(F32), (TB, TILE))
        for b in range(TB):
            seen[a * TB + b] = observed[b : b + 1, :]
        for code in range(NBR):
            hit = jnp.max(jnp.where(live == code, 1.0, 0.0).astype(F32), axis=1, keepdims=True)
            hit = jnp.broadcast_to(hit, (TB, TILE))
            for b in range(TB):
                present[code, a * TB + b] = hit[b : b + 1, :]
    for r in range(1, len(reaches) - 1):
        hear(r)
        announce(r + 1)

    to_right.wait()
    to_left.wait()
    for row in range(TA + 2):
        tile_row = jnp.clip(chan * TA + row - 1, 0, chans * TA - 1)
        for col, (source, side) in enumerate(
            ((w_left, 1), (w_own, 0), (w_own, 1), (w_right, 0))
        ):
            w_ext[col, row] = source[tile_row * TB + side].astype(BF16).astype(F32)
    w_part[...] = jnp.zeros_like(w_part)
    for t in range(TILES):
        w_part[t : t + 1, :] = w_ext[1 + t % TB, 1 + t // TB]
    cent[TILES * NCH :, :] = w_part[...].astype(BF16)
    w_line = jnp.concatenate([w_own[chan * TILES + t] for t in range(TILES)], axis=1)
    acc[...] = jnp.zeros_like(acc)
    w_acc[...] = jnp.zeros_like(w_acc)

    for i in range(chans - 1):
        sky_copy(i).wait_send()
        remote(
            recv.at[behind[i]],
            recv.at[behind[i]],
            sky_send.at[i],
            sky_recv.at[i],
            behind[i],
            patch,
        ).wait_recv()

    gathered = recv[...].reshape(NCH, BLOCK)
    cleaned = lax.dot_general(
        project,
        gathered,
        (((1,), (0,)), ((), ())),
        precision=HIGHEST,
        preferred_element_type=F32,
    )
    weighted32 = cleaned * w_line
    weighted = weighted32.astype(BF16)
    masked = jnp.concatenate(
        [weighted32[:, t * TILE : (t + 1) * TILE] * seen[t] for t in range(TILES)], axis=1
    ).astype(BF16)
    part = lax.dot_general(masked, weighted, NT, preferred_element_type=F32)
    half = NCH // 2
    packed = jnp.concatenate([part[:half], part[half:]], axis=1)
    total = jnp.sum(seen[...], axis=0) * TILE
    for row in range(half):
        piece[row, 0:1, :] = packed[row : row + 1, :]
    piece[:, 1:2, :] = jnp.broadcast_to(total[None], (half, 1, TILE))

    def seat_of(chan_list, n):
        i, c = seats[n]
        return chan_list[i] * CORES + cores[c]

    def plane_start(n, source, target, send, recv_sem):
        i, c = seats[n]
        copy = remote(
            source, target, send.at[n], recv_sem.at[n], ahead[i], z * CORES + cores[c]
        )
        copy.start()
        return copy

    def plane_wait(n, sent, target, send, recv_sem):
        i, c = seats[n]
        slot = target.at[seat_of(behind, n)]
        sent.wait_send()
        remote(
            slot, slot, send.at[n], recv_sem.at[n], behind[i], z * CORES + cores[c]
        ).wait_recv()

    plane_copies = [
        plane_start(n, piece.at[seat_of(ahead, n)], plane_in.at[seat], plane_send, plane_recv)
        for n in range(len(seats))
    ]

    plane_in[seat] = piece[seat]

    for t in range(TILES):
        tile = weighted[:, t * TILE : (t + 1) * TILE]
        ext[1 + t % TB, 1 + t // TB] = tile
        cent[t * NCH : (t + 1) * NCH, :] = tile

    side_copies = []
    for number, (dk, dp) in enumerate(SIDES):
        row_src, row_dst = span(dk, TA)
        col_src, col_dst = span(dp, TB)
        copy = remote(
            ext.at[col_src, row_src],
            ext.at[col_dst, row_dst],
            side_send.at[number],
            side_recv.at[number],
            (chan + dk + chans) % chans,
            (patch + dp + patches) % patches,
        )
        copy.start()
        side_copies.append(copy)


    @pl.loop(0, NBR)
    def _(code):
        centres = cent[...]
        for pair in range(NBIN // 2):
            lanes = slice(2 * pair * TILE, 2 * (pair + 1) * TILE)
            sums = jnp.dot(centres, mask[code, :, lanes], preferred_element_type=F32).astype(BF16)
            for half_bin in range(2):
                level = 2 * pair + half_bin
                cut = sums[:, half_bin * TILE : (half_bin + 1) * TILE]
                for t in range(TILES):
                    binned[
                        code,
                        level * NCH : (level + 1) * NCH,
                        t * TILE : (t + 1) * TILE,
                    ] = cut[t * NCH : (t + 1) * NCH, :]
                w_binned[code, :, level * TILE : (level + 1) * TILE] = cut[TILES * NCH :, :]

    for n in range(len(seats)):
        plane_wait(n, plane_copies[n], plane_in, plane_send, plane_recv)

    plane_sum = jnp.sum(plane_in[...], axis=0)
    z_out[...] = plane_sum
    z_in[z] = plane_sum

    steps = sorted(range(1, depth), key=lambda d: -min(d, depth - d))
    hear(len(reaches) - 1)
    z_copies = [
        remote(
            z_out, z_in.at[z], z_send.at[d], z_recv.at[d], *z_device((z + d) % depth)
        )
        for d in steps
    ]
    for copy in z_copies:
        copy.start()

    for copy in side_copies:
        copy.wait()

    @pl.loop(0, NBR)
    def _(code):
        row_shift = code // 3
        col_shift = code % 3
        parts = []
        for t in range(TILES):
            here = present[code, t]
            tile = ext[t % TB + col_shift, t // TB + row_shift]
            parts.append((tile.astype(F32) * here).astype(BF16))
            w_part[t : t + 1, :] = w_ext[t % TB + col_shift, t // TB + row_shift] * here
        partners = jnp.concatenate(parts, axis=1)
        acc[...] += lax.dot_general(binned[code], partners, NT, preferred_element_type=F32)
        w_tiles = w_part[0:8, :]
        w_acc[...] += w_binned[code].astype(F32)[0:8, :] * jnp.concatenate(
            [w_tiles] * NBIN, axis=1
        )

    for d, copy in zip(steps, z_copies):
        other = (z + depth - d) % depth
        copy.wait_send()
        remote(
            z_in.at[other], z_in.at[other], z_send.at[d], z_recv.at[d], *z_device(other)
        ).wait_recv()

    z_sum = jnp.sum(z_in[...], axis=0)
    whole_out[...] = z_sum
    whole_in[seat] = z_sum

    whole_copies = [
        plane_start(n, whole_out, whole_in.at[seat], whole_send, whole_recv)
        for n in range(len(seats))
    ]
    scales = []
    for level in range(NBIN):
        chunk = w_acc[:, level * TILE : (level + 1) * TILE]
        scales.append(
            jnp.maximum(jnp.sum(jnp.sum(chunk, axis=0, keepdims=True), axis=1, keepdims=True), 1.0)
        )
    for n in range(len(seats)):
        plane_wait(n, whole_copies[n], whole_in, whole_send, whole_recv)

    for row in range(half):
        packed_ref[row : row + 1, :] = whole_in[row, 0:1, :] / whole_in[row, 1:2, :]
    lines = packed_ref[...]
    covariance = jnp.concatenate([lines[:, :NCH], lines[:, NCH:]], axis=0)
    cov_out[...] = covariance
    only = covariance * identity()
    down = jnp.sqrt(jnp.sum(only, axis=1, keepdims=True) + 1e-06)
    across = jnp.sqrt(jnp.sum(only, axis=0, keepdims=True) + 1e-06)
    norm = down * across
    for level in range(NBIN):
        taper = 0.75 + 0.25 * math.cos(math.pi * level / NBIN)
        rows = acc[level * NCH : (level + 1) * NCH, :]
        corr[level] = taper * rows / (scales[level] * norm)


def per_device(sky_maps, mode_vectors, pixel_weight, neighbours, tile_counts, pair_bins):
    chans = lax.axis_size("chan")
    patches = lax.axis_size("patch")
    plane = chans * CORES
    depth = patches // CORES
    rows = chans * TILES
    weight = pixel_weight.reshape(rows, 1, TILE)
    dma = pltpu.SemaphoreType.DMA
    vmem = pltpu.VMEM
    anywhere = pl.BlockSpec(memory_space=pl.ANY)
    in_vmem = pl.BlockSpec(memory_space=pltpu.VMEM)
    correlation, covariance = pl.pallas_call(
        functools.partial(body, chans, patches),
        out_shape=(
            pltpu.VMEM((NBIN, NCH, NCH), F32),
            pltpu.VMEM((NCH, NCH), F32),
        ),
        in_specs=[anywhere] * 6,
        out_specs=(in_vmem, in_vmem),
        scratch_shapes=[
            vmem((chans, NCH // chans, BLOCK), F32),
            vmem((NCH // chans, chans * BLOCK), F32),
            vmem((MODES, NCH), F32),
            vmem((TA, TB, NBR), jnp.int32),
            vmem((TB, TA), jnp.int32),
            vmem((NBR, TILES, 1, TILE), F32),
            vmem((TILES, 1, TILE), F32),
            vmem((rows, 1, TILE), F32),
            vmem((rows, 1, TILE), F32),
            vmem((rows, 1, TILE), F32),
            vmem((NBR, TILE, TILE), jnp.int32),
            vmem((NBR, TILE, NBIN * TILE), BF16),
            vmem((TB + 2, TA + 2, NCH, TILE), BF16),
            vmem((TILES * NCH + 16, TILE), BF16),
            vmem((NBR, NBIN * NCH, BLOCK), BF16),
            vmem((NBR, 16, NBIN * TILE), BF16),
            vmem((TB + 2, TA + 2, 1, TILE), F32),
            vmem((16, TILE), F32),
            vmem((NBIN * NCH, NCH), F32),
            vmem((8, NBIN * TILE), F32),
            vmem((plane, 2, TILE), F32),
            vmem((plane, 2, TILE), F32),
            vmem((2, TILE), F32),
            vmem((depth, 2, TILE), F32),
            vmem((2, TILE), F32),
            vmem((plane, 2, TILE), F32),
            vmem((NCH // 2, TILE), F32),
            dma((6,)),
            dma((chans,)),
            dma((chans,)),
            dma((2,)),
            dma((2,)),
            dma((len(SIDES),)),
            dma((len(SIDES),)),
            dma((plane,)),
            dma((plane,)),
            dma((depth,)),
            dma((depth,)),
            dma((plane,)),
            dma((plane,)),
            pltpu.SemaphoreType.REGULAR((max(1, (depth // 2).bit_length() - 1),)),
        ],
        compiler_params=pltpu.CompilerParams(collective_id=0, has_side_effects=True),
        name="sky_pairs",
    )(sky_maps, mode_vectors.T, weight, neighbours, tile_counts.T, pair_bins)
    return (correlation[None, None], covariance)


def solution(mesh):
    return jax.shard_map(
        per_device,
        mesh=mesh,
        in_specs=(
            P("chan", "patch"),
            P(),
            P("patch"),
            P("chan", "patch", None),
            P("chan", "patch"),
            P(),
        ),
        out_specs=(P("chan", "patch", None, None, None), P()),
        check_vma=False,
    )
```

```python
import functools
import math

import jax
import jax.numpy as jnp
from jax import lax
from jax.experimental import pallas as pl
from jax.experimental.pallas import tpu as pltpu
from jax.sharding import PartitionSpec as P

NCH = 64
MODES = 8
TILE = 128
NBIN = 8
NBR = 9
TA = 3
TB = 2
TILES = TA * TB
BLOCK = TILES * TILE
CORES = 2
F32 = jnp.float32
BF16 = jnp.bfloat16
HIGHEST = lax.Precision.HIGHEST
MESH = pl.DeviceIdType.MESH
NT = (((1,), (1,)), ((), ()))
SIDES = [(dk, dp) for dk in (-1, 0, 1) for dp in (-1, 0, 1) if (dk, dp) != (0, 0)]


def remote(src, dst, send, recv, chan, patch):
    return pltpu.make_async_remote_copy(
        src_ref=src,
        dst_ref=dst,
        send_sem=send,
        recv_sem=recv,
        device_id=(chan, patch),
        device_id_type=MESH,
    )


def span(step, extent):
    if step > 0:
        return pl.ds(extent, 1), pl.ds(0, 1)
    if step < 0:
        return pl.ds(1, 1), pl.ds(extent + 1, 1)
    return pl.ds(1, extent), pl.ds(1, extent)


def project_matrix(modes):
    lane = lax.broadcasted_iota(jnp.int32, (NCH, MODES), 1)
    for number in range(MODES):
        column = modes[:, number : number + 1]
        column = column / jnp.sqrt(jnp.sum(column * column, axis=0, keepdims=True) + 1e-06)
        inner = jnp.sum(modes * column, axis=0, keepdims=True)
        later = jnp.where(lane > number, modes - inner * column, modes)
        modes = jnp.where(lane == number, column, later)
    outer = lax.dot_general(modes, modes, NT, precision=HIGHEST, preferred_element_type=F32)
    return identity() - outer


def identity():
    rows = lax.broadcasted_iota(jnp.int32, (NCH, NCH), 0)
    cols = lax.broadcasted_iota(jnp.int32, (NCH, NCH), 1)
    return jnp.where(rows == cols, 1.0, 0.0).astype(F32)


def body(
    chans,
    patches,
    sky,
    modes,
    weight,
    nbr,
    cnt,
    bins,
    corr,
    cov_out,
    recv,
    sky_in,
    modes_in,
    nbr_in,
    cnt_in,
    present,
    seen,
    w_own,
    w_left,
    w_right,
    table,
    mask,
    ext,
    cent,
    binned,
    w_binned,
    w_ext,
    w_part,
    acc,
    w_acc,
    piece,
    plane_in,
    z_out,
    z_in,
    whole_out,
    whole_in,
    packed_ref,
    local_sem,
    sky_send,
    sky_recv,
    w_send,
    w_recv,
    side_send,
    side_recv,
    plane_send,
    plane_recv,
    z_send,
    z_recv,
    whole_send,
    whole_recv,
    ready,
):
    depth = patches // CORES
    plane = chans * CORES
    side = math.isqrt(chans)
    chan = lax.axis_index("chan")
    patch = lax.axis_index("patch")
    z = patch // CORES
    core = patch % CORES
    seat = chan * CORES + core
    chan_y = chan // side
    chan_x = chan % side

    shifts = [(dy, dx) for dy in range(side) for dx in range(side)]
    shifts.sort(key=lambda d: -(min(d[0], side - d[0]) + min(d[1], side - d[1])))
    ahead = [(chan_y + dy) % side * side + (chan_x + dx) % side for dy, dx in shifts]
    behind = [
        (chan_y + side - dy) % side * side + (chan_x + side - dx) % side for dy, dx in shifts
    ]
    cores = (core, 1 - core)
    seats = [(i, c) for i in range(chans) for c in range(CORES) if (i, c) != (chans - 1, 0)]

    def z_device(other):
        return chan, other * CORES + core

    def signal(semaphore, device):
        pl.semaphore_signal(semaphore, inc=1, device_id=device, device_id_type=MESH)

    barrier = pltpu.get_barrier_semaphore()
    far = (patch + 2 * core - 1 + patches) % patches
    for shift in range(3):
        signal(barrier, ((chan + shift - 1 + chans) % chans, far))
    for i, c in seats:
        signal(barrier, (ahead[i], z * CORES + cores[c]))
    signal(barrier, z_device((z + 1) % depth))
    signal(barrier, z_device((z + depth - 1) % depth))

    def columns(other):
        return sky_in.at[:, pl.ds(pl.multiple_of(other * BLOCK, BLOCK), BLOCK)]

    local_copies = [
        pltpu.make_async_copy(source, target, local_sem.at[number])
        for number, (source, target) in enumerate(
            (
                (modes, modes_in),
                (bins, table),
                (nbr, nbr_in),
                (cnt, cnt_in),
                (weight, w_own),
                (sky, sky_in),
            )
        )
    ]
    for copy in local_copies:
        copy.start()

    local_copies[-1].wait()
    pl.semaphore_wait(barrier, 3 + len(seats) + 2)

    def sky_copy(i):
        return remote(
            columns(ahead[i]), recv.at[chan], sky_send.at[i], sky_recv.at[i], ahead[i], patch
        )

    for i in range(chans - 1):
        sky_copy(i).start()

    right = (patch + 1) % patches
    left = (patch + patches - 1) % patches
    to_right = remote(weight, w_left, w_send.at[0], w_recv.at[0], chan, right)
    to_left = remote(weight, w_right, w_send.at[1], w_recv.at[1], chan, left)
    to_right.start()
    to_left.start()

    reaches = [1 << r for r in range((depth // 2).bit_length() - 1)]

    def announce(r):
        signal(ready.at[r], z_device((z + reaches[r]) % depth))
        signal(ready.at[r], z_device((z + depth - reaches[r]) % depth))

    def hear(r):
        pl.semaphore_wait(ready.at[r], 2)

    announce(0)
    recv[chan] = sky_in[:, pl.ds(pl.multiple_of(chan * BLOCK, BLOCK), BLOCK)]
    for copy in local_copies[:-1]:
        copy.wait()

    project = project_matrix(modes_in[...].T)
    hear(0)
    announce(1)

    @pl.loop(0, NBR)
    def _(code):
        bins_here = table[code]
        for level in range(NBIN):
            mask[code, :, level * TILE : (level + 1) * TILE] = jnp.where(
                bins_here == level, 1.0, 0.0
            ).astype(BF16)

    slots = lax.broadcasted_iota(jnp.int32, (TB, NBR), 1)
    for a in range(TA):
        count = cnt_in[:, a : a + 1]
        live = jnp.where(slots < count, nbr_in[a], NBR)
        observed = jnp.broadcast_to(jnp.where(count > 0, 1.0, 0.0).astype(F32), (TB, TILE))
        for b in range(TB):
            seen[a * TB + b] = observed[b : b + 1, :]
        for code in range(NBR):
            hit = jnp.max(jnp.where(live == code, 1.0, 0.0).astype(F32), axis=1, keepdims=True)
            hit = jnp.broadcast_to(hit, (TB, TILE))
            for b in range(TB):
                present[code, a * TB + b] = hit[b : b + 1, :]
    for r in range(1, len(reaches) - 1):
        hear(r)
        announce(r + 1)

    to_right.wait()
    to_left.wait()
    for row in range(TA + 2):
        tile_row = jnp.clip(chan * TA + row - 1, 0, chans * TA - 1)
        for col, (source, edge) in enumerate(
            ((w_left, 1), (w_own, 0), (w_own, 1), (w_right, 0))
        ):
            w_ext[col, row] = source[tile_row * TB + edge].astype(BF16).astype(F32)
    w_part[...] = jnp.zeros_like(w_part)
    for t in range(TILES):
        w_part[t : t + 1, :] = w_ext[1 + t % TB, 1 + t // TB]
    cent[TILES * NCH :, :] = w_part[...].astype(BF16)
    w_line = jnp.concatenate([w_own[chan * TILES + t] for t in range(TILES)], axis=1)
    acc[...] = jnp.zeros_like(acc)
    w_acc[...] = jnp.zeros_like(w_acc)

    for i in range(chans - 1):
        sky_copy(i).wait_send()
        remote(
            recv.at[behind[i]],
            recv.at[behind[i]],
            sky_send.at[i],
            sky_recv.at[i],
            behind[i],
            patch,
        ).wait_recv()

    gathered = recv[...].reshape(NCH, BLOCK)
    cleaned = lax.dot_general(
        project,
        gathered,
        (((1,), (0,)), ((), ())),
        precision=HIGHEST,
        preferred_element_type=F32,
    )
    weighted32 = cleaned * w_line
    weighted = weighted32.astype(BF16)
    masked = jnp.concatenate(
        [weighted32[:, t * TILE : (t + 1) * TILE] * seen[t] for t in range(TILES)], axis=1
    ).astype(BF16)
    part = lax.dot_general(masked, weighted, NT, preferred_element_type=F32)
    half = NCH // 2
    pieces = side * CORES
    lines = half // pieces
    packed = jnp.concatenate([part[:half], part[half:]], axis=1)
    total = jnp.sum(seen[...], axis=0) * TILE
    for number in range(pieces):
        piece[number, 0:lines, :] = packed[number * lines : (number + 1) * lines, :]
        piece[number, lines : lines + 1, :] = total

    def seat_of(chan_list, n):
        i, c = seats[n]
        return chan_list[i] * CORES + cores[c]

    def piece_of(chan_list, n):
        i, c = seats[n]
        return chan_list[i] % side * CORES + cores[c]

    own_piece = chan_x * CORES + core

    def plane_start(n, source, target, send, recv_sem):
        i, c = seats[n]
        copy = remote(
            source, target, send.at[n], recv_sem.at[n], ahead[i], z * CORES + cores[c]
        )
        copy.start()
        return copy

    def plane_wait(n, sent, target, slot_of, send, recv_sem):
        i, c = seats[n]
        slot = target.at[slot_of(behind, n)]
        sent.wait_send()
        remote(
            slot, slot, send.at[n], recv_sem.at[n], behind[i], z * CORES + cores[c]
        ).wait_recv()

    plane_copies = [
        plane_start(n, piece.at[piece_of(ahead, n)], plane_in.at[seat], plane_send, plane_recv)
        for n in range(len(seats))
    ]

    plane_in[seat] = piece[own_piece]

    for t in range(TILES):
        tile = weighted[:, t * TILE : (t + 1) * TILE]
        ext[1 + t % TB, 1 + t // TB] = tile
        cent[t * NCH : (t + 1) * NCH, :] = tile

    side_copies = []
    for number, (dk, dp) in enumerate(SIDES):
        row_src, row_dst = span(dk, TA)
        col_src, col_dst = span(dp, TB)
        copy = remote(
            ext.at[col_src, row_src],
            ext.at[col_dst, row_dst],
            side_send.at[number],
            side_recv.at[number],
            (chan + dk + chans) % chans,
            (patch + dp + patches) % patches,
        )
        copy.start()
        side_copies.append(copy)


    @pl.loop(0, NBR)
    def _(code):
        centres = cent[...]
        for pair in range(NBIN // 2):
            lanes = slice(2 * pair * TILE, 2 * (pair + 1) * TILE)
            sums = jnp.dot(centres, mask[code, :, lanes], preferred_element_type=F32).astype(BF16)
            for half_bin in range(2):
                level = 2 * pair + half_bin
                cut = sums[:, half_bin * TILE : (half_bin + 1) * TILE]
                for t in range(TILES):
                    binned[
                        code,
                        level * NCH : (level + 1) * NCH,
                        t * TILE : (t + 1) * TILE,
                    ] = cut[t * NCH : (t + 1) * NCH, :]
                w_binned[code, :, level * TILE : (level + 1) * TILE] = cut[TILES * NCH :, :]

    for n in range(len(seats)):
        plane_wait(n, plane_copies[n], plane_in, seat_of, plane_send, plane_recv)

    plane_sum = jnp.sum(plane_in[...], axis=0)
    z_out[...] = plane_sum
    z_in[z] = plane_sum

    steps = sorted(range(1, depth), key=lambda d: -min(d, depth - d))
    hear(len(reaches) - 1)
    z_copies = [
        remote(
            z_out, z_in.at[z], z_send.at[d], z_recv.at[d], *z_device((z + d) % depth)
        )
        for d in steps
    ]
    for copy in z_copies:
        copy.start()

    for copy in side_copies:
        copy.wait()

    @pl.loop(0, NBR)
    def _(code):
        row_shift = code // 3
        col_shift = code % 3
        parts = []
        for t in range(TILES):
            here = present[code, t]
            tile = ext[t % TB + col_shift, t // TB + row_shift]
            parts.append((tile.astype(F32) * here).astype(BF16))
            w_part[t : t + 1, :] = w_ext[t % TB + col_shift, t // TB + row_shift] * here
        partners = jnp.concatenate(parts, axis=1)
        acc[...] += lax.dot_general(binned[code], partners, NT, preferred_element_type=F32)
        w_tiles = w_part[0:8, :]
        w_acc[...] += w_binned[code].astype(F32)[0:8, :] * jnp.concatenate(
            [w_tiles] * NBIN, axis=1
        )

    for d, copy in zip(steps, z_copies):
        other = (z + depth - d) % depth
        copy.wait_send()
        remote(
            z_in.at[other], z_in.at[other], z_send.at[d], z_recv.at[d], *z_device(other)
        ).wait_recv()

    z_sum = jnp.sum(z_in[...], axis=0)
    whole_out[...] = z_sum
    whole_in[own_piece] = z_sum

    row_seats = [n for n, (i, c) in enumerate(seats) if shifts[i][0] == 0]
    whole_copies = [
        plane_start(n, whole_out, whole_in.at[own_piece], whole_send, whole_recv)
        for n in row_seats
    ]
    scales = []
    for level in range(NBIN):
        chunk = w_acc[:, level * TILE : (level + 1) * TILE]
        scales.append(
            jnp.maximum(jnp.sum(jnp.sum(chunk, axis=0, keepdims=True), axis=1, keepdims=True), 1.0)
        )
    for n, copy in zip(row_seats, whole_copies):
        plane_wait(n, copy, whole_in, piece_of, whole_send, whole_recv)

    for number in range(pieces):
        packed_ref[number * lines : (number + 1) * lines, :] = (
            whole_in[number, 0:lines, :] / whole_in[number, lines : lines + 1, :]
        )
    merged = packed_ref[...]
    covariance = jnp.concatenate([merged[:, :NCH], merged[:, NCH:]], axis=0)
    cov_out[...] = covariance
    only = covariance * identity()
    down = jnp.sqrt(jnp.sum(only, axis=1, keepdims=True) + 1e-06)
    across = jnp.sqrt(jnp.sum(only, axis=0, keepdims=True) + 1e-06)
    norm = down * across
    for level in range(NBIN):
        taper = 0.75 + 0.25 * math.cos(math.pi * level / NBIN)
        rows = acc[level * NCH : (level + 1) * NCH, :]
        corr[level] = taper * rows / (scales[level] * norm)


def per_device(sky_maps, mode_vectors, pixel_weight, neighbours, tile_counts, pair_bins):
    chans = lax.axis_size("chan")
    patches = lax.axis_size("patch")
    plane = chans * CORES
    depth = patches // CORES
    rows = chans * TILES
    pieces = math.isqrt(chans) * CORES
    lines = NCH // 2 // pieces + 1
    weight = pixel_weight.reshape(rows, 1, TILE)
    dma = pltpu.SemaphoreType.DMA
    vmem = pltpu.VMEM
    anywhere = pl.BlockSpec(memory_space=pl.ANY)
    in_vmem = pl.BlockSpec(memory_space=pltpu.VMEM)
    correlation, covariance = pl.pallas_call(
        functools.partial(body, chans, patches),
        out_shape=(
            pltpu.VMEM((NBIN, NCH, NCH), F32),
            pltpu.VMEM((NCH, NCH), F32),
        ),
        in_specs=[anywhere] * 6,
        out_specs=(in_vmem, in_vmem),
        scratch_shapes=[
            vmem((chans, NCH // chans, BLOCK), F32),
            vmem((NCH // chans, chans * BLOCK), F32),
            vmem((MODES, NCH), F32),
            vmem((TA, TB, NBR), jnp.int32),
            vmem((TB, TA), jnp.int32),
            vmem((NBR, TILES, 1, TILE), F32),
            vmem((TILES, 1, TILE), F32),
            vmem((rows, 1, TILE), F32),
            vmem((rows, 1, TILE), F32),
            vmem((rows, 1, TILE), F32),
            vmem((NBR, TILE, TILE), jnp.int32),
            vmem((NBR, TILE, NBIN * TILE), BF16),
            vmem((TB + 2, TA + 2, NCH, TILE), BF16),
            vmem((TILES * NCH + 16, TILE), BF16),
            vmem((NBR, NBIN * NCH, BLOCK), BF16),
            vmem((NBR, 16, NBIN * TILE), BF16),
            vmem((TB + 2, TA + 2, 1, TILE), F32),
            vmem((16, TILE), F32),
            vmem((NBIN * NCH, NCH), F32),
            vmem((8, NBIN * TILE), F32),
            vmem((pieces, lines, TILE), F32),
            vmem((plane, lines, TILE), F32),
            vmem((lines, TILE), F32),
            vmem((depth, lines, TILE), F32),
            vmem((lines, TILE), F32),
            vmem((pieces, lines, TILE), F32),
            vmem((NCH // 2, TILE), F32),
            dma((6,)),
            dma((chans,)),
            dma((chans,)),
            dma((2,)),
            dma((2,)),
            dma((len(SIDES),)),
            dma((len(SIDES),)),
            dma((plane,)),
            dma((plane,)),
            dma((depth,)),
            dma((depth,)),
            dma((plane,)),
            dma((plane,)),
            pltpu.SemaphoreType.REGULAR((max(1, (depth // 2).bit_length() - 1),)),
        ],
        compiler_params=pltpu.CompilerParams(collective_id=0, has_side_effects=True),
        name="sky_pairs",
    )(sky_maps, mode_vectors.T, weight, neighbours, tile_counts.T, pair_bins)
    return (correlation[None, None], covariance)


def solution(mesh):
    return jax.shard_map(
        per_device,
        mesh=mesh,
        in_specs=(
            P("chan", "patch"),
            P(),
            P("patch"),
            P("chan", "patch", None),
            P("chan", "patch"),
            P(),
        ),
        out_specs=(P("chan", "patch", None, None, None), P()),
        check_vma=False,
    )
```

```python
import functools
import math

import jax
import jax.numpy as jnp
from jax import lax
from jax.experimental import pallas as pl
from jax.experimental.pallas import tpu as pltpu
from jax.sharding import PartitionSpec as P

NCH = 64
MODES = 8
TILE = 128
NBIN = 8
NBR = 9
TA = 3
TB = 2
TILES = TA * TB
BLOCK = TILES * TILE
CORES = 2
F32 = jnp.float32
BF16 = jnp.bfloat16
HIGHEST = lax.Precision.HIGHEST
MESH = pl.DeviceIdType.MESH
NT = (((1,), (1,)), ((), ()))
SIDES = [(dk, dp) for dk in (-1, 0, 1) for dp in (-1, 0, 1) if (dk, dp) != (0, 0)]


def remote(src, dst, send, recv, chan, patch):
    return pltpu.make_async_remote_copy(
        src_ref=src,
        dst_ref=dst,
        send_sem=send,
        recv_sem=recv,
        device_id=(chan, patch),
        device_id_type=MESH,
    )


def span(step, extent):
    if step > 0:
        return pl.ds(extent, 1), pl.ds(0, 1)
    if step < 0:
        return pl.ds(1, 1), pl.ds(extent + 1, 1)
    return pl.ds(1, extent), pl.ds(1, extent)


def project_matrix(modes):
    lane = lax.broadcasted_iota(jnp.int32, (NCH, MODES), 1)
    for number in range(MODES):
        column = modes[:, number : number + 1]
        column = column / jnp.sqrt(jnp.sum(column * column, axis=0, keepdims=True) + 1e-06)
        inner = jnp.sum(modes * column, axis=0, keepdims=True)
        later = jnp.where(lane > number, modes - inner * column, modes)
        modes = jnp.where(lane == number, column, later)
    outer = lax.dot_general(modes, modes, NT, precision=HIGHEST, preferred_element_type=F32)
    return identity() - outer


def identity():
    rows = lax.broadcasted_iota(jnp.int32, (NCH, NCH), 0)
    cols = lax.broadcasted_iota(jnp.int32, (NCH, NCH), 1)
    return jnp.where(rows == cols, 1.0, 0.0).astype(F32)


def body(
    chans,
    patches,
    sky,
    modes,
    weight,
    nbr,
    cnt,
    bins,
    corr,
    cov_out,
    recv,
    sky_in,
    modes_in,
    nbr_in,
    cnt_in,
    present,
    seen,
    w_own,
    w_left,
    w_right,
    table,
    mask,
    ext,
    cent,
    binned,
    w_binned,
    w_ext,
    w_part,
    acc,
    w_acc,
    piece,
    plane_in,
    z_out,
    z_in,
    whole_out,
    whole_in,
    packed_ref,
    local_sem,
    sky_send,
    sky_recv,
    w_send,
    w_recv,
    side_send,
    side_recv,
    plane_send,
    plane_recv,
    z_send,
    z_recv,
    whole_send,
    whole_recv,
    ready,
):
    depth = patches // CORES
    plane = chans * CORES
    side = math.isqrt(chans)
    chan = lax.axis_index("chan")
    patch = lax.axis_index("patch")
    z = patch // CORES
    core = patch % CORES
    seat = chan * CORES + core
    chan_y = chan // side
    chan_x = chan % side

    shifts = [(dy, dx) for dy in range(side) for dx in range(side)]
    shifts.sort(key=lambda d: -(min(d[0], side - d[0]) + min(d[1], side - d[1])))
    ahead = [(chan_y + dy) % side * side + (chan_x + dx) % side for dy, dx in shifts]
    behind = [
        (chan_y + side - dy) % side * side + (chan_x + side - dx) % side for dy, dx in shifts
    ]
    cores = (core, 1 - core)
    seats = [(i, c) for i in range(chans) for c in range(CORES) if (i, c) != (chans - 1, 0)]

    def z_device(other):
        return chan, other * CORES + core

    def signal(semaphore, device):
        pl.semaphore_signal(semaphore, inc=1, device_id=device, device_id_type=MESH)

    barrier = pltpu.get_barrier_semaphore()
    far = (patch + 2 * core - 1 + patches) % patches
    for shift in range(3):
        signal(barrier, ((chan + shift - 1 + chans) % chans, far))
    for i, c in seats:
        signal(barrier, (ahead[i], z * CORES + cores[c]))
    signal(barrier, z_device((z + 1) % depth))
    signal(barrier, z_device((z + depth - 1) % depth))

    def columns(other):
        return sky_in.at[:, pl.ds(pl.multiple_of(other * BLOCK, BLOCK), BLOCK)]

    local_copies = [
        pltpu.make_async_copy(source, target, local_sem.at[number])
        for number, (source, target) in enumerate(
            (
                (modes, modes_in),
                (bins, table),
                (nbr, nbr_in),
                (cnt, cnt_in),
                (weight, w_own),
                (sky, sky_in),
            )
        )
    ]
    for copy in local_copies:
        copy.start()

    local_copies[-1].wait()
    pl.semaphore_wait(barrier, 3 + len(seats) + 2)

    def sky_copy(i):
        return remote(
            columns(ahead[i]), recv.at[chan], sky_send.at[i], sky_recv.at[i], ahead[i], patch
        )

    for i in range(chans - 1):
        sky_copy(i).start()

    right = (patch + 1) % patches
    left = (patch + patches - 1) % patches
    to_right = remote(weight, w_left, w_send.at[0], w_recv.at[0], chan, right)
    to_left = remote(weight, w_right, w_send.at[1], w_recv.at[1], chan, left)
    to_right.start()
    to_left.start()

    reaches = [1 << r for r in range((depth // 2).bit_length() - 1)]

    def announce(r):
        signal(ready.at[r], z_device((z + reaches[r]) % depth))
        signal(ready.at[r], z_device((z + depth - reaches[r]) % depth))

    def hear(r):
        pl.semaphore_wait(ready.at[r], 2)

    announce(0)
    recv[chan] = sky_in[:, pl.ds(pl.multiple_of(chan * BLOCK, BLOCK), BLOCK)]
    for copy in local_copies[:-1]:
        copy.wait()

    project = project_matrix(modes_in[...].T)
    hear(0)
    announce(1)

    @pl.loop(0, NBR)
    def _(code):
        bins_here = table[code]
        for level in range(NBIN):
            mask[code, :, level * TILE : (level + 1) * TILE] = jnp.where(
                bins_here == level, 1.0, 0.0
            ).astype(BF16)

    slots = lax.broadcasted_iota(jnp.int32, (TB, NBR), 1)
    for a in range(TA):
        count = cnt_in[:, a : a + 1]
        live = jnp.where(slots < count, nbr_in[a], NBR)
        observed = jnp.broadcast_to(jnp.where(count > 0, 1.0, 0.0).astype(F32), (TB, TILE))
        for b in range(TB):
            seen[a * TB + b] = observed[b : b + 1, :]
        for code in range(NBR):
            hit = jnp.max(jnp.where(live == code, 1.0, 0.0).astype(F32), axis=1, keepdims=True)
            hit = jnp.broadcast_to(hit, (TB, TILE))
            for b in range(TB):
                present[code, a * TB + b] = hit[b : b + 1, :]
    for r in range(1, len(reaches) - 1):
        hear(r)
        announce(r + 1)

    to_right.wait()
    to_left.wait()
    for row in range(TA + 2):
        tile_row = jnp.clip(chan * TA + row - 1, 0, chans * TA - 1)
        for col, (source, edge) in enumerate(
            ((w_left, 1), (w_own, 0), (w_own, 1), (w_right, 0))
        ):
            w_ext[col, row] = source[tile_row * TB + edge].astype(BF16).astype(F32)
    w_part[...] = jnp.zeros_like(w_part)
    for t in range(TILES):
        w_part[t : t + 1, :] = w_ext[1 + t % TB, 1 + t // TB]
    cent[TILES * NCH :, :] = w_part[...].astype(BF16)
    w_line = jnp.concatenate([w_own[chan * TILES + t] for t in range(TILES)], axis=1)
    acc[...] = jnp.zeros_like(acc)
    w_acc[...] = jnp.zeros_like(w_acc)

    for i in range(chans - 1):
        sky_copy(i).wait_send()
        remote(
            recv.at[behind[i]],
            recv.at[behind[i]],
            sky_send.at[i],
            sky_recv.at[i],
            behind[i],
            patch,
        ).wait_recv()

    gathered = recv[...].reshape(NCH, BLOCK)
    cleaned = lax.dot_general(
        project,
        gathered,
        (((1,), (0,)), ((), ())),
        precision=HIGHEST,
        preferred_element_type=F32,
    )
    weighted32 = cleaned * w_line
    weighted = weighted32.astype(BF16)
    masked = jnp.concatenate(
        [weighted32[:, t * TILE : (t + 1) * TILE] * seen[t] for t in range(TILES)], axis=1
    ).astype(BF16)
    part = lax.dot_general(masked, weighted, NT, preferred_element_type=F32)
    half = NCH // 2
    quarter = half // 2
    pieces = 2 * CORES
    lines = quarter // pieces
    below = lax.broadcasted_iota(jnp.int32, (half, half), 0)
    beside = lax.broadcasted_iota(jnp.int32, (half, half), 1)
    first, cross, second = part[:half, :half], part[:half, half:], part[half:, half:]
    corner = jnp.where(beside <= below, first, second)
    folded = jnp.concatenate([cross, corner], axis=1)
    packed = jnp.concatenate([folded[:quarter], folded[quarter:]], axis=1)
    second_diagonal = jnp.sum(jnp.where(beside == below, second, 0.0), axis=0, keepdims=True)
    total = jnp.sum(seen[...], axis=0) * TILE
    extra = jnp.concatenate([second_diagonal, total[:, half:]], axis=1)
    for number in range(pieces):
        piece[number, 0:lines, :] = packed[number * lines : (number + 1) * lines, :]
        piece[number, lines : lines + 1, :] = extra

    def seat_of(chan_list, n):
        i, c = seats[n]
        return chan_list[i] * CORES + cores[c]

    def piece_of(chan_list, n):
        i, c = seats[n]
        return chan_list[i] % 2 * CORES + cores[c]

    own_piece = chan_x % 2 * CORES + core

    def plane_start(n, source, target, send, recv_sem):
        i, c = seats[n]
        copy = remote(
            source, target, send.at[n], recv_sem.at[n], ahead[i], z * CORES + cores[c]
        )
        copy.start()
        return copy

    def plane_wait(n, sent, target, slot_of, send, recv_sem):
        i, c = seats[n]
        slot = target.at[slot_of(behind, n)]
        sent.wait_send()
        remote(
            slot, slot, send.at[n], recv_sem.at[n], behind[i], z * CORES + cores[c]
        ).wait_recv()

    plane_copies = [
        plane_start(n, piece.at[piece_of(ahead, n)], plane_in.at[seat], plane_send, plane_recv)
        for n in range(len(seats))
    ]

    plane_in[seat] = piece[own_piece]

    for t in range(TILES):
        tile = weighted[:, t * TILE : (t + 1) * TILE]
        ext[1 + t % TB, 1 + t // TB] = tile
        cent[t * NCH : (t + 1) * NCH, :] = tile

    side_copies = []
    for number, (dk, dp) in enumerate(SIDES):
        row_src, row_dst = span(dk, TA)
        col_src, col_dst = span(dp, TB)
        copy = remote(
            ext.at[col_src, row_src],
            ext.at[col_dst, row_dst],
            side_send.at[number],
            side_recv.at[number],
            (chan + dk + chans) % chans,
            (patch + dp + patches) % patches,
        )
        copy.start()
        side_copies.append(copy)


    @pl.loop(0, NBR)
    def _(code):
        centres = cent[...]
        for pair in range(NBIN // 2):
            lanes = slice(2 * pair * TILE, 2 * (pair + 1) * TILE)
            sums = jnp.dot(centres, mask[code, :, lanes], preferred_element_type=F32).astype(BF16)
            for half_bin in range(2):
                level = 2 * pair + half_bin
                cut = sums[:, half_bin * TILE : (half_bin + 1) * TILE]
                for t in range(TILES):
                    binned[
                        code,
                        level * NCH : (level + 1) * NCH,
                        t * TILE : (t + 1) * TILE,
                    ] = cut[t * NCH : (t + 1) * NCH, :]
                w_binned[code, :, level * TILE : (level + 1) * TILE] = cut[TILES * NCH :, :]

    for n in range(len(seats)):
        plane_wait(n, plane_copies[n], plane_in, seat_of, plane_send, plane_recv)

    plane_sum = jnp.sum(plane_in[...], axis=0)
    z_out[...] = plane_sum
    z_in[z] = plane_sum

    steps = sorted(range(1, depth), key=lambda d: -min(d, depth - d))
    hear(len(reaches) - 1)
    z_copies = [
        remote(
            z_out, z_in.at[z], z_send.at[d], z_recv.at[d], *z_device((z + d) % depth)
        )
        for d in steps
    ]
    for copy in z_copies:
        copy.start()

    for copy in side_copies:
        copy.wait()

    @pl.loop(0, NBR)
    def _(code):
        row_shift = code // 3
        col_shift = code % 3
        parts = []
        for t in range(TILES):
            here = present[code, t]
            tile = ext[t % TB + col_shift, t // TB + row_shift]
            parts.append((tile.astype(F32) * here).astype(BF16))
            w_part[t : t + 1, :] = w_ext[t % TB + col_shift, t // TB + row_shift] * here
        partners = jnp.concatenate(parts, axis=1)
        acc[...] += lax.dot_general(binned[code], partners, NT, preferred_element_type=F32)
        w_tiles = w_part[0:8, :]
        w_acc[...] += w_binned[code].astype(F32)[0:8, :] * jnp.concatenate(
            [w_tiles] * NBIN, axis=1
        )

    for d, copy in zip(steps, z_copies):
        other = (z + depth - d) % depth
        copy.wait_send()
        remote(
            z_in.at[other], z_in.at[other], z_send.at[d], z_recv.at[d], *z_device(other)
        ).wait_recv()

    z_sum = jnp.sum(z_in[...], axis=0)
    whole_out[...] = z_sum
    whole_in[own_piece] = z_sum

    mate = chan + 1 - 2 * (chan_x % 2)
    mates = [(mate, 0), (mate, 1), (chan, 1)]

    def whole_copy(n, source, slot):
        other, c = mates[n]
        return remote(
            source, slot, whole_send.at[n], whole_recv.at[n], other, z * CORES + cores[c]
        )

    whole_copies = [whole_copy(n, whole_out, whole_in.at[own_piece]) for n in range(len(mates))]
    for copy in whole_copies:
        copy.start()
    scales = []
    for level in range(NBIN):
        chunk = w_acc[:, level * TILE : (level + 1) * TILE]
        scales.append(
            jnp.maximum(jnp.sum(jnp.sum(chunk, axis=0, keepdims=True), axis=1, keepdims=True), 1.0)
        )
        taper = 0.75 + 0.25 * math.cos(math.pi * level / NBIN)
        acc[level * NCH : (level + 1) * NCH, :] = (
            taper * acc[level * NCH : (level + 1) * NCH, :] / scales[level]
        )
    for n, copy in enumerate(whole_copies):
        other, c = mates[n]
        slot = whole_in.at[other % 2 * CORES + cores[c]]
        copy.wait_send()
        whole_copy(n, slot, slot).wait_recv()

    for number in range(pieces):
        packed_ref[number * lines : (number + 1) * lines, :] = (
            whole_in[number, 0:lines, :] / whole_in[number, lines : lines + 1, TILE - 1 :]
        )
    merged = packed_ref[...]
    unfolded = jnp.concatenate([merged[:, :NCH], merged[:, NCH:]], axis=0)
    cross, corner = unfolded[:, :half], unfolded[:, half:]
    turned = corner.T
    second_diagonal = (
        whole_in[0, lines : lines + 1, :half] / whole_in[0, lines : lines + 1, TILE - 1 :]
    )
    first = jnp.where(beside <= below, corner, turned)
    second = jnp.where(beside > below, corner, turned)
    second = jnp.where(beside == below, second_diagonal, second)
    covariance = jnp.concatenate(
        [
            jnp.concatenate([first, cross], axis=1),
            jnp.concatenate([cross.T, second], axis=1),
        ],
        axis=0,
    )
    cov_out[...] = covariance
    only = covariance * identity()
    down = jnp.sqrt(jnp.sum(only, axis=1, keepdims=True) + 1e-06)
    across = jnp.sqrt(jnp.sum(only, axis=0, keepdims=True) + 1e-06)
    inverse = 1.0 / (down * across)
    for level in range(NBIN):
        corr[level] = acc[level * NCH : (level + 1) * NCH, :] * inverse


def per_device(sky_maps, mode_vectors, pixel_weight, neighbours, tile_counts, pair_bins):
    chans = lax.axis_size("chan")
    patches = lax.axis_size("patch")
    plane = chans * CORES
    depth = patches // CORES
    rows = chans * TILES
    pieces = 2 * CORES
    lines = NCH // 4 // pieces + 1
    weight = pixel_weight.reshape(rows, 1, TILE)
    dma = pltpu.SemaphoreType.DMA
    vmem = pltpu.VMEM
    anywhere = pl.BlockSpec(memory_space=pl.ANY)
    in_vmem = pl.BlockSpec(memory_space=pltpu.VMEM)
    correlation, covariance = pl.pallas_call(
        functools.partial(body, chans, patches),
        out_shape=(
            pltpu.VMEM((NBIN, NCH, NCH), F32),
            pltpu.VMEM((NCH, NCH), F32),
        ),
        in_specs=[anywhere] * 6,
        out_specs=(in_vmem, in_vmem),
        scratch_shapes=[
            vmem((chans, NCH // chans, BLOCK), F32),
            vmem((NCH // chans, chans * BLOCK), F32),
            vmem((MODES, NCH), F32),
            vmem((TA, TB, NBR), jnp.int32),
            vmem((TB, TA), jnp.int32),
            vmem((NBR, TILES, 1, TILE), F32),
            vmem((TILES, 1, TILE), F32),
            vmem((rows, 1, TILE), F32),
            vmem((rows, 1, TILE), F32),
            vmem((rows, 1, TILE), F32),
            vmem((NBR, TILE, TILE), jnp.int32),
            vmem((NBR, TILE, NBIN * TILE), BF16),
            vmem((TB + 2, TA + 2, NCH, TILE), BF16),
            vmem((TILES * NCH + 16, TILE), BF16),
            vmem((NBR, NBIN * NCH, BLOCK), BF16),
            vmem((NBR, 16, NBIN * TILE), BF16),
            vmem((TB + 2, TA + 2, 1, TILE), F32),
            vmem((16, TILE), F32),
            vmem((NBIN * NCH, NCH), F32),
            vmem((8, NBIN * TILE), F32),
            vmem((pieces, lines, TILE), F32),
            vmem((plane, lines, TILE), F32),
            vmem((lines, TILE), F32),
            vmem((depth, lines, TILE), F32),
            vmem((lines, TILE), F32),
            vmem((pieces, lines, TILE), F32),
            vmem((NCH // 4, TILE), F32),
            dma((6,)),
            dma((chans,)),
            dma((chans,)),
            dma((2,)),
            dma((2,)),
            dma((len(SIDES),)),
            dma((len(SIDES),)),
            dma((plane,)),
            dma((plane,)),
            dma((depth,)),
            dma((depth,)),
            dma((3,)),
            dma((3,)),
            pltpu.SemaphoreType.REGULAR((max(1, (depth // 2).bit_length() - 1),)),
        ],
        compiler_params=pltpu.CompilerParams(collective_id=0, has_side_effects=True),
        name="sky_pairs",
    )(sky_maps, mode_vectors.T, weight, neighbours, tile_counts.T, pair_bins)
    return (correlation[None, None], covariance)


def solution(mesh):
    return jax.shard_map(
        per_device,
        mesh=mesh,
        in_specs=(
            P("chan", "patch"),
            P(),
            P("patch"),
            P("chan", "patch", None),
            P("chan", "patch"),
            P(),
        ),
        out_specs=(P("chan", "patch", None, None, None), P()),
        check_vma=False,
    )
```

```python
import functools
import math

import jax
import jax.numpy as jnp
from jax import lax
from jax.experimental import pallas as pl
from jax.experimental.pallas import tpu as pltpu
from jax.sharding import PartitionSpec as P

NCH = 64
MODES = 8
TILE = 128
NBIN = 8
NBR = 9
TA = 3
TB = 2
TILES = TA * TB
BLOCK = TILES * TILE
CORES = 2
F32 = jnp.float32
BF16 = jnp.bfloat16
HIGHEST = lax.Precision.HIGHEST
MESH = pl.DeviceIdType.MESH
NT = (((1,), (1,)), ((), ()))
SIDES = [(dk, dp) for dk in (-1, 0, 1) for dp in (-1, 0, 1) if (dk, dp) != (0, 0)]


def remote(src, dst, send, recv, chan, patch):
    return pltpu.make_async_remote_copy(
        src_ref=src,
        dst_ref=dst,
        send_sem=send,
        recv_sem=recv,
        device_id=(chan, patch),
        device_id_type=MESH,
    )


def span(step, extent):
    if step > 0:
        return pl.ds(extent, 1), pl.ds(0, 1)
    if step < 0:
        return pl.ds(1, 1), pl.ds(extent + 1, 1)
    return pl.ds(1, extent), pl.ds(1, extent)


def project_matrix(modes):
    lane = lax.broadcasted_iota(jnp.int32, (NCH, MODES), 1)
    for number in range(MODES):
        column = modes[:, number : number + 1]
        column = column / jnp.sqrt(jnp.sum(column * column, axis=0, keepdims=True) + 1e-06)
        inner = jnp.sum(modes * column, axis=0, keepdims=True)
        later = jnp.where(lane > number, modes - inner * column, modes)
        modes = jnp.where(lane == number, column, later)
    outer = lax.dot_general(modes, modes, NT, precision=HIGHEST, preferred_element_type=F32)
    return identity() - outer


def identity():
    rows = lax.broadcasted_iota(jnp.int32, (NCH, NCH), 0)
    cols = lax.broadcasted_iota(jnp.int32, (NCH, NCH), 1)
    return jnp.where(rows == cols, 1.0, 0.0).astype(F32)


def body(
    chans,
    patches,
    sky,
    modes,
    weight,
    nbr,
    cnt,
    bins,
    corr,
    cov_out,
    recv,
    sky_in,
    modes_in,
    nbr_in,
    cnt_in,
    present,
    seen,
    w_own,
    w_left,
    w_right,
    table,
    mask,
    ext,
    cent,
    binned,
    w_binned,
    w_ext,
    w_part,
    acc,
    w_acc,
    piece,
    plane_in,
    z_out,
    z_in,
    whole_out,
    whole_in,
    packed_ref,
    local_sem,
    sky_send,
    sky_recv,
    w_send,
    w_recv,
    side_send,
    side_recv,
    plane_send,
    plane_recv,
    z_send,
    z_recv,
    whole_send,
    whole_recv,
    ready,
):
    depth = patches // CORES
    plane = chans * CORES
    side = math.isqrt(chans)
    chan = lax.axis_index("chan")
    patch = lax.axis_index("patch")
    z = patch // CORES
    core = patch % CORES
    seat = chan * CORES + core
    chan_y = chan // side
    chan_x = chan % side

    shifts = [(dy, dx) for dy in range(side) for dx in range(side)]
    shifts.sort(key=lambda d: -(min(d[0], side - d[0]) + min(d[1], side - d[1])))
    ahead = [(chan_y + dy) % side * side + (chan_x + dx) % side for dy, dx in shifts]
    behind = [
        (chan_y + side - dy) % side * side + (chan_x + side - dx) % side for dy, dx in shifts
    ]
    cores = (core, 1 - core)
    seats = [(i, c) for i in range(chans) for c in range(CORES) if (i, c) != (chans - 1, 0)]

    def z_device(other):
        return chan, other * CORES + core

    def signal(semaphore, device):
        pl.semaphore_signal(semaphore, inc=1, device_id=device, device_id_type=MESH)

    barrier = pltpu.get_barrier_semaphore()
    far = (patch + 2 * core - 1 + patches) % patches
    for shift in range(3):
        signal(barrier, ((chan + shift - 1 + chans) % chans, far))
    for i, c in seats:
        signal(barrier, (ahead[i], z * CORES + cores[c]))
    signal(barrier, z_device((z + 1) % depth))
    signal(barrier, z_device((z + depth - 1) % depth))

    def columns(other):
        return sky_in.at[:, pl.ds(pl.multiple_of(other * BLOCK, BLOCK), BLOCK)]

    local_copies = [
        pltpu.make_async_copy(source, target, local_sem.at[number])
        for number, (source, target) in enumerate(
            (
                (modes, modes_in),
                (bins, table),
                (nbr, nbr_in),
                (cnt, cnt_in),
                (weight, w_own),
                (sky, sky_in),
            )
        )
    ]
    for copy in local_copies:
        copy.start()

    local_copies[-1].wait()
    pl.semaphore_wait(barrier, 3 + len(seats) + 2)

    def sky_copy(i):
        return remote(
            columns(ahead[i]), recv.at[chan], sky_send.at[i], sky_recv.at[i], ahead[i], patch
        )

    for i in range(chans - 1):
        sky_copy(i).start()

    right = (patch + 1) % patches
    left = (patch + patches - 1) % patches
    to_right = remote(weight, w_left, w_send.at[0], w_recv.at[0], chan, right)
    to_left = remote(weight, w_right, w_send.at[1], w_recv.at[1], chan, left)
    to_right.start()
    to_left.start()

    reaches = [1 << r for r in range((depth // 2).bit_length() - 1)]

    def announce(r):
        signal(ready.at[r], z_device((z + reaches[r]) % depth))
        signal(ready.at[r], z_device((z + depth - reaches[r]) % depth))

    def hear(r):
        pl.semaphore_wait(ready.at[r], 2)

    announce(0)
    recv[chan] = sky_in[:, pl.ds(pl.multiple_of(chan * BLOCK, BLOCK), BLOCK)]
    for copy in local_copies[:-1]:
        copy.wait()

    project = project_matrix(modes_in[...].T)
    hear(0)
    announce(1)

    @pl.loop(0, NBR)
    def _(code):
        bins_here = table[code]
        for level in range(NBIN):
            mask[code, :, level * TILE : (level + 1) * TILE] = jnp.where(
                bins_here == level, 1.0, 0.0
            ).astype(BF16)

    slots = lax.broadcasted_iota(jnp.int32, (TB, NBR), 1)
    for a in range(TA):
        count = cnt_in[:, a : a + 1]
        live = jnp.where(slots < count, nbr_in[a], NBR)
        observed = jnp.broadcast_to(jnp.where(count > 0, 1.0, 0.0).astype(F32), (TB, TILE))
        for b in range(TB):
            seen[a * TB + b] = observed[b : b + 1, :]
        for code in range(NBR):
            hit = jnp.max(jnp.where(live == code, 1.0, 0.0).astype(F32), axis=1, keepdims=True)
            hit = jnp.broadcast_to(hit, (TB, TILE))
            for b in range(TB):
                present[code, a * TB + b] = hit[b : b + 1, :]
    for r in range(1, len(reaches) - 1):
        hear(r)
        announce(r + 1)

    to_right.wait()
    to_left.wait()
    for row in range(TA + 2):
        tile_row = jnp.clip(chan * TA + row - 1, 0, chans * TA - 1)
        for col, (source, edge) in enumerate(
            ((w_left, 1), (w_own, 0), (w_own, 1), (w_right, 0))
        ):
            w_ext[col, row] = source[tile_row * TB + edge].astype(BF16).astype(F32)
    w_part[...] = jnp.zeros_like(w_part)
    for t in range(TILES):
        w_part[t : t + 1, :] = w_ext[1 + t % TB, 1 + t // TB]
    cent[TILES * NCH :, :] = w_part[...].astype(BF16)
    w_line = jnp.concatenate([w_own[chan * TILES + t] for t in range(TILES)], axis=1)
    acc[...] = jnp.zeros_like(acc)
    w_acc[...] = jnp.zeros_like(w_acc)

    for i in range(chans - 1):
        sky_copy(i).wait_send()
        remote(
            recv.at[behind[i]],
            recv.at[behind[i]],
            sky_send.at[i],
            sky_recv.at[i],
            behind[i],
            patch,
        ).wait_recv()

    gathered = recv[...].reshape(NCH, BLOCK)
    cleaned = lax.dot_general(
        project,
        gathered,
        (((1,), (0,)), ((), ())),
        precision=HIGHEST,
        preferred_element_type=F32,
    )
    weighted32 = cleaned * w_line
    weighted = weighted32.astype(BF16)
    masked = jnp.concatenate(
        [weighted32[:, t * TILE : (t + 1) * TILE] * seen[t] for t in range(TILES)], axis=1
    ).astype(BF16)
    part = lax.dot_general(masked, weighted, NT, preferred_element_type=F32)
    half = NCH // 2
    quarter = half // 2
    pieces = 2 * CORES
    lines = quarter // pieces
    below = lax.broadcasted_iota(jnp.int32, (half, half), 0)
    beside = lax.broadcasted_iota(jnp.int32, (half, half), 1)
    first, cross, second = part[:half, :half], part[:half, half:], part[half:, half:]
    corner = jnp.where(beside <= below, first, second)
    folded = jnp.concatenate([cross, corner], axis=1)
    packed = jnp.concatenate([folded[:quarter], folded[quarter:]], axis=1)
    second_diagonal = jnp.sum(jnp.where(beside == below, second, 0.0), axis=0, keepdims=True)
    total = jnp.sum(seen[...], axis=0) * TILE
    extra = jnp.concatenate([second_diagonal, total[:, half:]], axis=1)
    for number in range(pieces):
        piece[number, 0:lines, :] = packed[number * lines : (number + 1) * lines, :]
        piece[number, lines : lines + 1, :] = extra

    def seat_of(chan_list, n):
        i, c = seats[n]
        return chan_list[i] * CORES + cores[c]

    def piece_of(chan_list, n):
        i, c = seats[n]
        return chan_list[i] % 2 * CORES + cores[c]

    own_piece = chan_x % 2 * CORES + core

    def plane_start(n, source, target, send, recv_sem):
        i, c = seats[n]
        copy = remote(
            source, target, send.at[n], recv_sem.at[n], ahead[i], z * CORES + cores[c]
        )
        copy.start()
        return copy

    def plane_wait(n, sent, target, slot_of, send, recv_sem):
        i, c = seats[n]
        slot = target.at[slot_of(behind, n)]
        sent.wait_send()
        remote(
            slot, slot, send.at[n], recv_sem.at[n], behind[i], z * CORES + cores[c]
        ).wait_recv()

    plane_copies = [
        plane_start(n, piece.at[piece_of(ahead, n)], plane_in.at[seat], plane_send, plane_recv)
        for n in range(len(seats))
    ]

    plane_in[seat] = piece[own_piece]

    for t in range(TILES):
        tile = weighted[:, t * TILE : (t + 1) * TILE]
        ext[1 + t % TB, 1 + t // TB] = tile
        cent[t * NCH : (t + 1) * NCH, :] = tile

    side_copies = []
    for number, (dk, dp) in enumerate(SIDES):
        row_src, row_dst = span(dk, TA)
        col_src, col_dst = span(dp, TB)
        copy = remote(
            ext.at[col_src, row_src],
            ext.at[col_dst, row_dst],
            side_send.at[number],
            side_recv.at[number],
            (chan + dk + chans) % chans,
            (patch + dp + patches) % patches,
        )
        copy.start()
        side_copies.append(copy)


    @pl.loop(0, NBR)
    def _(code):
        centres = cent[...]
        for pair in range(NBIN // 2):
            lanes = slice(2 * pair * TILE, 2 * (pair + 1) * TILE)
            sums = jnp.dot(centres, mask[code, :, lanes], preferred_element_type=F32).astype(BF16)
            for half_bin in range(2):
                level = 2 * pair + half_bin
                cut = sums[:, half_bin * TILE : (half_bin + 1) * TILE]
                for t in range(TILES):
                    binned[
                        code,
                        level * NCH : (level + 1) * NCH,
                        t * TILE : (t + 1) * TILE,
                    ] = cut[t * NCH : (t + 1) * NCH, :]
                w_binned[code, :, level * TILE : (level + 1) * TILE] = cut[TILES * NCH :, :]

    for n in range(len(seats)):
        plane_wait(n, plane_copies[n], plane_in, seat_of, plane_send, plane_recv)

    plane_sum = jnp.sum(plane_in[...], axis=0)
    z_out[...] = plane_sum
    z_in[z] = plane_sum

    steps = sorted(range(1, depth), key=lambda d: -min(d, depth - d))
    hear(len(reaches) - 1)
    z_copies = [
        remote(
            z_out, z_in.at[z], z_send.at[d], z_recv.at[d], *z_device((z + d) % depth)
        )
        for d in steps
    ]
    for copy in z_copies:
        copy.start()

    for copy in side_copies:
        copy.wait()

    @pl.loop(0, NBR)
    def _(code):
        row_shift = code // 3
        col_shift = code % 3
        parts = []
        for t in range(TILES):
            here = present[code, t]
            tile = ext[t % TB + col_shift, t // TB + row_shift]
            parts.append((tile.astype(F32) * here).astype(BF16))
            w_part[t : t + 1, :] = w_ext[t % TB + col_shift, t // TB + row_shift] * here
        partners = jnp.concatenate(parts, axis=1)
        acc[...] += lax.dot_general(binned[code], partners, NT, preferred_element_type=F32)
        w_tiles = w_part[0:8, :]
        w_acc[...] += w_binned[code].astype(F32)[0:8, :] * jnp.concatenate(
            [w_tiles] * NBIN, axis=1
        )

    for d, copy in zip(steps, z_copies):
        other = (z + depth - d) % depth
        copy.wait_send()
        remote(
            z_in.at[other], z_in.at[other], z_send.at[d], z_recv.at[d], *z_device(other)
        ).wait_recv()

    z_sum = jnp.sum(z_in[...], axis=0)
    whole_out[...] = z_sum
    whole_in[own_piece] = z_sum

    mate = chan + 1 - 2 * (chan_x % 2)
    mates = [(mate, 0), (mate, 1), (chan, 1)]

    def whole_copy(n, source, slot):
        other, c = mates[n]
        return remote(
            source, slot, whole_send.at[n], whole_recv.at[n], other, z * CORES + cores[c]
        )

    whole_copies = [whole_copy(n, whole_out, whole_in.at[own_piece]) for n in range(len(mates))]
    for copy in whole_copies:
        copy.start()
    scales = []
    for level in range(NBIN):
        chunk = w_acc[:, level * TILE : (level + 1) * TILE]
        scales.append(
            jnp.maximum(jnp.sum(jnp.sum(chunk, axis=0, keepdims=True), axis=1, keepdims=True), 1.0)
        )
        taper = 0.75 + 0.25 * math.cos(math.pi * level / NBIN)
        acc[level * NCH : (level + 1) * NCH, :] = (
            taper * acc[level * NCH : (level + 1) * NCH, :] / scales[level]
        )
    for n, copy in enumerate(whole_copies):
        other, c = mates[n]
        slot = whole_in.at[other % 2 * CORES + cores[c]]
        copy.wait_send()
        whole_copy(n, slot, slot).wait_recv()

    for number in range(pieces):
        packed_ref[number * lines : (number + 1) * lines, :] = (
            whole_in[number, 0:lines, :] / whole_in[number, lines : lines + 1, TILE - 1 :]
        )
    merged = packed_ref[...]
    unfolded = jnp.concatenate([merged[:, :NCH], merged[:, NCH:]], axis=0)
    cross, corner = unfolded[:, :half], unfolded[:, half:]
    turned = corner.T
    second_diagonal = (
        whole_in[0, lines : lines + 1, :half] / whole_in[0, lines : lines + 1, TILE - 1 :]
    )
    first = jnp.where(beside <= below, corner, turned)
    second = jnp.where(beside > below, corner, turned)
    second = jnp.where(beside == below, second_diagonal, second)
    covariance = jnp.concatenate(
        [
            jnp.concatenate([first, cross], axis=1),
            jnp.concatenate([cross.T, second], axis=1),
        ],
        axis=0,
    )
    cov_out[...] = covariance
    only = covariance * identity()
    down = jnp.sqrt(jnp.sum(only, axis=1, keepdims=True) + 1e-06)
    across = jnp.sqrt(jnp.sum(only, axis=0, keepdims=True) + 1e-06)
    inverse = 1.0 / (down * across)
    for level in range(NBIN):
        corr[level] = acc[level * NCH : (level + 1) * NCH, :] * inverse


def deliver(corr_in, cov_in, corr_out, cov_out, sems):
    copies = [
        pltpu.make_async_copy(corr_in, corr_out, sems.at[0]),
        pltpu.make_async_copy(cov_in, cov_out, sems.at[1]),
    ]
    for copy in copies:
        copy.start()
    for copy in copies:
        copy.wait()


def per_device(sky_maps, mode_vectors, pixel_weight, neighbours, tile_counts, pair_bins):
    chans = lax.axis_size("chan")
    patches = lax.axis_size("patch")
    plane = chans * CORES
    depth = patches // CORES
    rows = chans * TILES
    pieces = 2 * CORES
    lines = NCH // 4 // pieces + 1
    weight = pixel_weight.reshape(rows, 1, TILE)
    dma = pltpu.SemaphoreType.DMA
    vmem = pltpu.VMEM
    anywhere = pl.BlockSpec(memory_space=pl.ANY)
    in_vmem = pl.BlockSpec(memory_space=pltpu.VMEM)
    correlation, covariance = pl.pallas_call(
        functools.partial(body, chans, patches),
        out_shape=(
            pltpu.VMEM((NBIN, NCH, NCH), F32),
            pltpu.VMEM((NCH, NCH), F32),
        ),
        in_specs=[anywhere] * 6,
        out_specs=(in_vmem, in_vmem),
        scratch_shapes=[
            vmem((chans, NCH // chans, BLOCK), F32),
            vmem((NCH // chans, chans * BLOCK), F32),
            vmem((MODES, NCH), F32),
            vmem((TA, TB, NBR), jnp.int32),
            vmem((TB, TA), jnp.int32),
            vmem((NBR, TILES, 1, TILE), F32),
            vmem((TILES, 1, TILE), F32),
            vmem((rows, 1, TILE), F32),
            vmem((rows, 1, TILE), F32),
            vmem((rows, 1, TILE), F32),
            vmem((NBR, TILE, TILE), jnp.int32),
            vmem((NBR, TILE, NBIN * TILE), BF16),
            vmem((TB + 2, TA + 2, NCH, TILE), BF16),
            vmem((TILES * NCH + 16, TILE), BF16),
            vmem((NBR, NBIN * NCH, BLOCK), BF16),
            vmem((NBR, 16, NBIN * TILE), BF16),
            vmem((TB + 2, TA + 2, 1, TILE), F32),
            vmem((16, TILE), F32),
            vmem((NBIN * NCH, NCH), F32),
            vmem((8, NBIN * TILE), F32),
            vmem((pieces, lines, TILE), F32),
            vmem((plane, lines, TILE), F32),
            vmem((lines, TILE), F32),
            vmem((depth, lines, TILE), F32),
            vmem((lines, TILE), F32),
            vmem((pieces, lines, TILE), F32),
            vmem((NCH // 4, TILE), F32),
            dma((6,)),
            dma((chans,)),
            dma((chans,)),
            dma((2,)),
            dma((2,)),
            dma((len(SIDES),)),
            dma((len(SIDES),)),
            dma((plane,)),
            dma((plane,)),
            dma((depth,)),
            dma((depth,)),
            dma((3,)),
            dma((3,)),
            pltpu.SemaphoreType.REGULAR((max(1, (depth // 2).bit_length() - 1),)),
        ],
        compiler_params=pltpu.CompilerParams(collective_id=0, has_side_effects=True),
        name="sky_pairs",
    )(sky_maps, mode_vectors.T, weight, neighbours, tile_counts.T, pair_bins)
    correlation, covariance = pl.pallas_call(
        deliver,
        out_shape=(
            jax.ShapeDtypeStruct((NBIN, NCH, NCH), F32),
            jax.ShapeDtypeStruct((NCH, NCH), F32),
        ),
        in_specs=[in_vmem, in_vmem],
        out_specs=(anywhere, anywhere),
        scratch_shapes=[dma((2,))],
        name="deliver",
    )(
        pltpu.with_memory_space_constraint(correlation, pltpu.VMEM),
        pltpu.with_memory_space_constraint(covariance, pltpu.VMEM),
    )
    return (correlation[None, None], covariance)


def solution(mesh):
    return jax.shard_map(
        per_device,
        mesh=mesh,
        in_specs=(
            P("chan", "patch"),
            P(),
            P("patch"),
            P("chan", "patch", None),
            P("chan", "patch"),
            P(),
        ),
        out_specs=(P("chan", "patch", None, None, None), P()),
        check_vma=False,
    )
```

```python
import functools
import math

import jax
import jax.numpy as jnp
from jax import lax
from jax.experimental import pallas as pl
from jax.experimental.pallas import tpu as pltpu
from jax.sharding import PartitionSpec as P

NCH = 64
MODES = 8
TILE = 128
NBIN = 8
NBR = 9
TA = 3
TB = 2
TILES = TA * TB
BLOCK = TILES * TILE
CORES = 2
F32 = jnp.float32
BF16 = jnp.bfloat16
HIGHEST = lax.Precision.HIGHEST
MESH = pl.DeviceIdType.MESH
NT = (((1,), (1,)), ((), ()))
SIDES = [(dk, dp) for dk in (-1, 0, 1) for dp in (-1, 0, 1) if (dk, dp) != (0, 0)]


def remote(src, dst, send, recv, chan, patch):
    return pltpu.make_async_remote_copy(
        src_ref=src,
        dst_ref=dst,
        send_sem=send,
        recv_sem=recv,
        device_id=(chan, patch),
        device_id_type=MESH,
    )


def span(step, extent):
    if step > 0:
        return pl.ds(extent, 1), pl.ds(0, 1)
    if step < 0:
        return pl.ds(1, 1), pl.ds(extent + 1, 1)
    return pl.ds(1, extent), pl.ds(1, extent)


def project_matrix(modes):
    lane = lax.broadcasted_iota(jnp.int32, (NCH, MODES), 1)
    for number in range(MODES):
        column = modes[:, number : number + 1]
        column = column / jnp.sqrt(jnp.sum(column * column, axis=0, keepdims=True) + 1e-06)
        inner = jnp.sum(modes * column, axis=0, keepdims=True)
        later = jnp.where(lane > number, modes - inner * column, modes)
        modes = jnp.where(lane == number, column, later)
    outer = lax.dot_general(modes, modes, NT, precision=HIGHEST, preferred_element_type=F32)
    return identity() - outer


def identity():
    rows = lax.broadcasted_iota(jnp.int32, (NCH, NCH), 0)
    cols = lax.broadcasted_iota(jnp.int32, (NCH, NCH), 1)
    return jnp.where(rows == cols, 1.0, 0.0).astype(F32)


def body(
    chans,
    patches,
    sky,
    modes,
    weight,
    nbr,
    cnt,
    bins,
    corr,
    cov_out,
    recv,
    sky_in,
    modes_in,
    nbr_in,
    cnt_in,
    present,
    seen,
    w_own,
    w_left,
    w_right,
    table,
    mask,
    ext,
    cent,
    binned,
    w_binned,
    w_ext,
    w_part,
    acc,
    w_acc,
    piece,
    plane_in,
    z_out,
    z_in,
    whole_out,
    whole_in,
    packed_ref,
    local_sem,
    sky_send,
    sky_recv,
    w_send,
    w_recv,
    side_send,
    side_recv,
    plane_send,
    plane_recv,
    z_send,
    z_recv,
    whole_send,
    whole_recv,
    ready,
):
    depth = patches // CORES
    plane = chans * CORES
    side = math.isqrt(chans)
    chan = lax.axis_index("chan")
    patch = lax.axis_index("patch")
    z = patch // CORES
    core = patch % CORES
    seat = chan * CORES + core
    chan_y = chan // side
    chan_x = chan % side

    shifts = [(dy, dx) for dy in range(side) for dx in range(side)]
    shifts.sort(key=lambda d: -(min(d[0], side - d[0]) + min(d[1], side - d[1])))
    ahead = [(chan_y + dy) % side * side + (chan_x + dx) % side for dy, dx in shifts]
    behind = [
        (chan_y + side - dy) % side * side + (chan_x + side - dx) % side for dy, dx in shifts
    ]
    cores = (core, 1 - core)
    seats = [(i, c) for i in range(chans) for c in range(CORES) if (i, c) != (chans - 1, 0)]

    def z_device(other):
        return chan, other * CORES + core

    def signal(semaphore, device):
        pl.semaphore_signal(semaphore, inc=1, device_id=device, device_id_type=MESH)

    barrier = pltpu.get_barrier_semaphore()
    far = (patch + 2 * core - 1 + patches) % patches
    for shift in range(3):
        signal(barrier, ((chan + shift - 1 + chans) % chans, far))
    for i, c in seats:
        signal(barrier, (ahead[i], z * CORES + cores[c]))
    signal(barrier, z_device((z + 1) % depth))
    signal(barrier, z_device((z + depth - 1) % depth))

    def columns(other):
        return sky_in.at[:, pl.ds(pl.multiple_of(other * BLOCK, BLOCK), BLOCK)]

    local_copies = [
        pltpu.make_async_copy(source, target, local_sem.at[number])
        for number, (source, target) in enumerate(
            (
                (modes, modes_in),
                (bins, table),
                (nbr, nbr_in),
                (cnt, cnt_in),
                (weight, w_own),
                (sky, sky_in),
            )
        )
    ]
    for copy in local_copies:
        copy.start()

    local_copies[-1].wait()
    pl.semaphore_wait(barrier, 3 + len(seats) + 2)

    def sky_copy(i):
        return remote(
            columns(ahead[i]), recv.at[chan], sky_send.at[i], sky_recv.at[i], ahead[i], patch
        )

    for i in range(chans - 1):
        sky_copy(i).start()

    right = (patch + 1) % patches
    left = (patch + patches - 1) % patches
    to_right = remote(weight, w_left, w_send.at[0], w_recv.at[0], chan, right)
    to_left = remote(weight, w_right, w_send.at[1], w_recv.at[1], chan, left)
    to_right.start()
    to_left.start()

    reaches = [1 << r for r in range((depth // 2).bit_length() - 1)]

    def announce(r):
        signal(ready.at[r], z_device((z + reaches[r]) % depth))
        signal(ready.at[r], z_device((z + depth - reaches[r]) % depth))

    def hear(r):
        pl.semaphore_wait(ready.at[r], 2)

    announce(0)
    recv[chan] = sky_in[:, pl.ds(pl.multiple_of(chan * BLOCK, BLOCK), BLOCK)]
    for copy in local_copies[:-1]:
        copy.wait()

    project = project_matrix(modes_in[...].T)
    hear(0)
    announce(1)

    @pl.loop(0, NBR)
    def _(code):
        bins_here = table[code]
        for level in range(NBIN):
            mask[code, :, level * TILE : (level + 1) * TILE] = jnp.where(
                bins_here == level, 1.0, 0.0
            ).astype(BF16)

    slots = lax.broadcasted_iota(jnp.int32, (TB, NBR), 1)
    for a in range(TA):
        count = cnt_in[:, a : a + 1]
        live = jnp.where(slots < count, nbr_in[a], NBR)
        observed = jnp.broadcast_to(jnp.where(count > 0, 1.0, 0.0).astype(F32), (TB, TILE))
        for b in range(TB):
            seen[a * TB + b] = observed[b : b + 1, :]
        for code in range(NBR):
            hit = jnp.max(jnp.where(live == code, 1.0, 0.0).astype(F32), axis=1, keepdims=True)
            hit = jnp.broadcast_to(hit, (TB, TILE))
            for b in range(TB):
                present[code, a * TB + b] = hit[b : b + 1, :]
    for r in range(1, len(reaches) - 1):
        hear(r)
        announce(r + 1)

    to_right.wait()
    to_left.wait()
    for row in range(TA + 2):
        tile_row = jnp.clip(chan * TA + row - 1, 0, chans * TA - 1)
        for col, (source, edge) in enumerate(
            ((w_left, 1), (w_own, 0), (w_own, 1), (w_right, 0))
        ):
            w_ext[col, row] = source[tile_row * TB + edge].astype(BF16).astype(F32)
    w_part[...] = jnp.zeros_like(w_part)
    for t in range(TILES):
        w_part[t : t + 1, :] = w_ext[1 + t % TB, 1 + t // TB]
    cent[TILES * NCH :, :] = w_part[...].astype(BF16)
    w_line = jnp.concatenate([w_own[chan * TILES + t] for t in range(TILES)], axis=1)
    acc[...] = jnp.zeros_like(acc)
    w_acc[...] = jnp.zeros_like(w_acc)

    for i in range(chans - 1):
        remote(
            recv.at[behind[i]],
            recv.at[behind[i]],
            sky_send.at[i],
            sky_recv.at[i],
            behind[i],
            patch,
        ).wait_recv()

    gathered = recv[...].reshape(NCH, BLOCK)
    cleaned = lax.dot_general(
        project,
        gathered,
        (((1,), (0,)), ((), ())),
        precision=HIGHEST,
        preferred_element_type=F32,
    )
    weighted32 = cleaned * w_line
    weighted = weighted32.astype(BF16)
    masked = jnp.concatenate(
        [weighted32[:, t * TILE : (t + 1) * TILE] * seen[t] for t in range(TILES)], axis=1
    ).astype(BF16)
    part = lax.dot_general(masked, weighted, NT, preferred_element_type=F32)
    half = NCH // 2
    quarter = half // 2
    pieces = 2 * CORES
    lines = quarter // pieces
    below = lax.broadcasted_iota(jnp.int32, (half, half), 0)
    beside = lax.broadcasted_iota(jnp.int32, (half, half), 1)
    first, cross, second = part[:half, :half], part[:half, half:], part[half:, half:]
    corner = jnp.where(beside <= below, first, second)
    folded = jnp.concatenate([cross, corner], axis=1)
    packed = jnp.concatenate([folded[:quarter], folded[quarter:]], axis=1)
    second_diagonal = jnp.sum(jnp.where(beside == below, second, 0.0), axis=0, keepdims=True)
    total = jnp.sum(seen[...], axis=0) * TILE
    extra = jnp.concatenate([second_diagonal, total[:, half:]], axis=1)
    for number in range(pieces):
        piece[number, 0:lines, :] = packed[number * lines : (number + 1) * lines, :]
        piece[number, lines : lines + 1, :] = extra

    def seat_of(chan_list, n):
        i, c = seats[n]
        return chan_list[i] * CORES + cores[c]

    def piece_of(chan_list, n):
        i, c = seats[n]
        return chan_list[i] % 2 * CORES + cores[c]

    own_piece = chan_x % 2 * CORES + core

    def plane_start(n, source, target, send, recv_sem):
        i, c = seats[n]
        copy = remote(
            source, target, send.at[n], recv_sem.at[n], ahead[i], z * CORES + cores[c]
        )
        copy.start()
        return copy

    def plane_wait(n, target, slot_of, send, recv_sem):
        i, c = seats[n]
        slot = target.at[slot_of(behind, n)]
        remote(
            slot, slot, send.at[n], recv_sem.at[n], behind[i], z * CORES + cores[c]
        ).wait_recv()

    plane_copies = [
        plane_start(n, piece.at[piece_of(ahead, n)], plane_in.at[seat], plane_send, plane_recv)
        for n in range(len(seats))
    ]

    plane_in[seat] = piece[own_piece]

    for t in range(TILES):
        tile = weighted[:, t * TILE : (t + 1) * TILE]
        ext[1 + t % TB, 1 + t // TB] = tile
        cent[t * NCH : (t + 1) * NCH, :] = tile

    side_copies = []
    for number, (dk, dp) in enumerate(SIDES):
        row_src, row_dst = span(dk, TA)
        col_src, col_dst = span(dp, TB)
        copy = remote(
            ext.at[col_src, row_src],
            ext.at[col_dst, row_dst],
            side_send.at[number],
            side_recv.at[number],
            (chan + dk + chans) % chans,
            (patch + dp + patches) % patches,
        )
        copy.start()
        side_copies.append(copy)


    @pl.loop(0, NBR)
    def _(code):
        centres = cent[...]
        for pair in range(NBIN // 2):
            lanes = slice(2 * pair * TILE, 2 * (pair + 1) * TILE)
            sums = jnp.dot(centres, mask[code, :, lanes], preferred_element_type=F32).astype(BF16)
            for half_bin in range(2):
                level = 2 * pair + half_bin
                cut = sums[:, half_bin * TILE : (half_bin + 1) * TILE]
                for t in range(TILES):
                    binned[
                        code,
                        level * NCH : (level + 1) * NCH,
                        t * TILE : (t + 1) * TILE,
                    ] = cut[t * NCH : (t + 1) * NCH, :]
                w_binned[code, :, level * TILE : (level + 1) * TILE] = cut[TILES * NCH :, :]

    for i in range(chans - 1):
        sky_copy(i).wait_send()
    for n in range(len(seats)):
        plane_wait(n, plane_in, seat_of, plane_send, plane_recv)

    plane_sum = jnp.sum(plane_in[...], axis=0)
    z_out[...] = plane_sum
    z_in[z] = plane_sum

    steps = sorted(range(1, depth), key=lambda d: -min(d, depth - d))
    hear(len(reaches) - 1)
    z_copies = [
        remote(
            z_out, z_in.at[z], z_send.at[d], z_recv.at[d], *z_device((z + d) % depth)
        )
        for d in steps
    ]
    for copy in z_copies:
        copy.start()

    for copy in plane_copies:
        copy.wait_send()
    for copy in side_copies:
        copy.wait()

    @pl.loop(0, NBR)
    def _(code):
        row_shift = code // 3
        col_shift = code % 3
        parts = []
        for t in range(TILES):
            here = present[code, t]
            tile = ext[t % TB + col_shift, t // TB + row_shift]
            parts.append((tile.astype(F32) * here).astype(BF16))
            w_part[t : t + 1, :] = w_ext[t % TB + col_shift, t // TB + row_shift] * here
        partners = jnp.concatenate(parts, axis=1)
        acc[...] += lax.dot_general(binned[code], partners, NT, preferred_element_type=F32)
        w_tiles = w_part[0:8, :]
        w_acc[...] += w_binned[code].astype(F32)[0:8, :] * jnp.concatenate(
            [w_tiles] * NBIN, axis=1
        )

    for d in steps:
        other = (z + depth - d) % depth
        remote(
            z_in.at[other], z_in.at[other], z_send.at[d], z_recv.at[d], *z_device(other)
        ).wait_recv()

    z_sum = jnp.sum(z_in[...], axis=0)
    whole_out[...] = z_sum
    whole_in[own_piece] = z_sum

    mate = chan + 1 - 2 * (chan_x % 2)
    mates = [(mate, 0), (mate, 1), (chan, 1)]

    def whole_copy(n, source, slot):
        other, c = mates[n]
        return remote(
            source, slot, whole_send.at[n], whole_recv.at[n], other, z * CORES + cores[c]
        )

    whole_copies = [whole_copy(n, whole_out, whole_in.at[own_piece]) for n in range(len(mates))]
    for copy in whole_copies:
        copy.start()
    scales = []
    for level in range(NBIN):
        chunk = w_acc[:, level * TILE : (level + 1) * TILE]
        scales.append(
            jnp.maximum(jnp.sum(jnp.sum(chunk, axis=0, keepdims=True), axis=1, keepdims=True), 1.0)
        )
        taper = 0.75 + 0.25 * math.cos(math.pi * level / NBIN)
        acc[level * NCH : (level + 1) * NCH, :] = (
            taper * acc[level * NCH : (level + 1) * NCH, :] / scales[level]
        )
    for copy in z_copies:
        copy.wait_send()
    for n, copy in enumerate(whole_copies):
        other, c = mates[n]
        slot = whole_in.at[other % 2 * CORES + cores[c]]
        copy.wait_send()
        whole_copy(n, slot, slot).wait_recv()

    for number in range(pieces):
        packed_ref[number * lines : (number + 1) * lines, :] = (
            whole_in[number, 0:lines, :] / whole_in[number, lines : lines + 1, TILE - 1 :]
        )
    merged = packed_ref[...]
    unfolded = jnp.concatenate([merged[:, :NCH], merged[:, NCH:]], axis=0)
    cross, corner = unfolded[:, :half], unfolded[:, half:]
    turned = corner.T
    second_diagonal = (
        whole_in[0, lines : lines + 1, :half] / whole_in[0, lines : lines + 1, TILE - 1 :]
    )
    first = jnp.where(beside <= below, corner, turned)
    second = jnp.where(beside > below, corner, turned)
    second = jnp.where(beside == below, second_diagonal, second)
    covariance = jnp.concatenate(
        [
            jnp.concatenate([first, cross], axis=1),
            jnp.concatenate([cross.T, second], axis=1),
        ],
        axis=0,
    )
    cov_out[...] = covariance
    only = covariance * identity()
    down = jnp.sqrt(jnp.sum(only, axis=1, keepdims=True) + 1e-06)
    across = jnp.sqrt(jnp.sum(only, axis=0, keepdims=True) + 1e-06)
    inverse = 1.0 / (down * across)
    for level in range(NBIN):
        corr[level] = acc[level * NCH : (level + 1) * NCH, :] * inverse


def deliver(corr_in, cov_in, corr_out, cov_out, sems):
    copies = [
        pltpu.make_async_copy(corr_in, corr_out, sems.at[0]),
        pltpu.make_async_copy(cov_in, cov_out, sems.at[1]),
    ]
    for copy in copies:
        copy.start()
    for copy in copies:
        copy.wait()


def per_device(sky_maps, mode_vectors, pixel_weight, neighbours, tile_counts, pair_bins):
    chans = lax.axis_size("chan")
    patches = lax.axis_size("patch")
    plane = chans * CORES
    depth = patches // CORES
    rows = chans * TILES
    pieces = 2 * CORES
    lines = NCH // 4 // pieces + 1
    weight = pixel_weight.reshape(rows, 1, TILE)
    dma = pltpu.SemaphoreType.DMA
    vmem = pltpu.VMEM
    anywhere = pl.BlockSpec(memory_space=pl.ANY)
    in_vmem = pl.BlockSpec(memory_space=pltpu.VMEM)
    correlation, covariance = pl.pallas_call(
        functools.partial(body, chans, patches),
        out_shape=(
            pltpu.VMEM((NBIN, NCH, NCH), F32),
            pltpu.VMEM((NCH, NCH), F32),
        ),
        in_specs=[anywhere] * 6,
        out_specs=(in_vmem, in_vmem),
        scratch_shapes=[
            vmem((chans, NCH // chans, BLOCK), F32),
            vmem((NCH // chans, chans * BLOCK), F32),
            vmem((MODES, NCH), F32),
            vmem((TA, TB, NBR), jnp.int32),
            vmem((TB, TA), jnp.int32),
            vmem((NBR, TILES, 1, TILE), F32),
            vmem((TILES, 1, TILE), F32),
            vmem((rows, 1, TILE), F32),
            vmem((rows, 1, TILE), F32),
            vmem((rows, 1, TILE), F32),
            vmem((NBR, TILE, TILE), jnp.int32),
            vmem((NBR, TILE, NBIN * TILE), BF16),
            vmem((TB + 2, TA + 2, NCH, TILE), BF16),
            vmem((TILES * NCH + 16, TILE), BF16),
            vmem((NBR, NBIN * NCH, BLOCK), BF16),
            vmem((NBR, 16, NBIN * TILE), BF16),
            vmem((TB + 2, TA + 2, 1, TILE), F32),
            vmem((16, TILE), F32),
            vmem((NBIN * NCH, NCH), F32),
            vmem((8, NBIN * TILE), F32),
            vmem((pieces, lines, TILE), F32),
            vmem((plane, lines, TILE), F32),
            vmem((lines, TILE), F32),
            vmem((depth, lines, TILE), F32),
            vmem((lines, TILE), F32),
            vmem((pieces, lines, TILE), F32),
            vmem((NCH // 4, TILE), F32),
            dma((6,)),
            dma((chans,)),
            dma((chans,)),
            dma((2,)),
            dma((2,)),
            dma((len(SIDES),)),
            dma((len(SIDES),)),
            dma((plane,)),
            dma((plane,)),
            dma((depth,)),
            dma((depth,)),
            dma((3,)),
            dma((3,)),
            pltpu.SemaphoreType.REGULAR((max(1, (depth // 2).bit_length() - 1),)),
        ],
        compiler_params=pltpu.CompilerParams(collective_id=0, has_side_effects=True),
        name="sky_pairs",
    )(sky_maps, mode_vectors.T, weight, neighbours, tile_counts.T, pair_bins)
    correlation, covariance = pl.pallas_call(
        deliver,
        out_shape=(
            jax.ShapeDtypeStruct((NBIN, NCH, NCH), F32),
            jax.ShapeDtypeStruct((NCH, NCH), F32),
        ),
        in_specs=[in_vmem, in_vmem],
        out_specs=(anywhere, anywhere),
        scratch_shapes=[dma((2,))],
        name="deliver",
    )(
        pltpu.with_memory_space_constraint(correlation, pltpu.VMEM),
        pltpu.with_memory_space_constraint(covariance, pltpu.VMEM),
    )
    return (correlation[None, None], covariance)


def solution(mesh):
    return jax.shard_map(
        per_device,
        mesh=mesh,
        in_specs=(
            P("chan", "patch"),
            P(),
            P("patch"),
            P("chan", "patch", None),
            P("chan", "patch"),
            P(),
        ),
        out_specs=(P("chan", "patch", None, None, None), P()),
        check_vma=False,
    )
```
